32 devices in a mesh: dp: 8 (over z, x), tensor: 4 (over y, core).
Axes of the slice: x: 2, y: 2, z: 4, core: 2. Of those that a mesh axis runs over, the one named last changes fastest.
Arguments:
- inputs: bfloat16 [2048, 8192], P('dp', 'tensor'), may hold values from -6 to 6
- out_grads: bfloat16 [2048, 8192], P('dp', 'tensor'), may hold values from -6 to 6
- gate_pre: bfloat16 [2048, 28672], P('dp', 'tensor'), may hold values from -6 to 6
- up_pre: bfloat16 [2048, 28672], P('dp', 'tensor'), may hold values from -6 to 6
- hidden_grad: bfloat16 [2048, 28672], P('dp', 'tensor'), may hold values from -6 to 6
- proj_model: bfloat16 [8192, 128], P(('tensor', 'dp')), may hold values from -0.0625 to 0.0625
- proj_hidden: bfloat16 [28672, 192], P(('tensor', 'dp')), may hold values from -0.03125 to 0.03125
- lengths: int32 [8, 4], P('dp'), may hold values from 1 to 192, 256 in all within a row
- owners: int32 [8, 4], P('dp'), may hold values from 0 to 3, each once within a row
Outputs:
- features: float32 [32, 12288], P(('dp', 'tensor'))
The draws below stay inside these ranges and needn't reach their ends.
Inputs may be any that keep to these rules, and one draw needn't show every extreme that they name: `lengths`: each row sums to 256, and each row has an example of exactly 192 tokens. `owners`: each row names every slot once.
All inputs are finite; a program needn't handle non-finite values.
Results may differ from the reference program's by a relative error of at most 0.0029.
Values may be sent and summed in bfloat16 or wider, within the bound.
A program may use at most 64 MiB of HBM per device.

```python
import math
import jax
import jax.numpy as jnp
import numpy as np
from jax import lax

D = 8192
FF = 28672
RANK = 64
TOK_DEV = 256
MOST = 192
TOKENS = 2048
EXAMPLES = 32
FEAT = 12288
N_DP = 8
N_TENSOR = 4


def level_of(key, extent, pieces, low, largest):
    def one(axis_at, shards_of):
        steps = jax.random.uniform(jax.random.fold_in(jax.random.fold_in(key, 6), axis_at), (shards_of,), jnp.float32, low / len(pieces), largest / len(pieces))
        return jnp.repeat(jnp.exp(steps), extent[axis_at] // shards_of).reshape((-1,) + (1,) * (len(extent) - axis_at - 1))

    level = one(*pieces[0])
    for cut in pieces[1:]:
        level = level * one(*cut)
    return level


def length_profile(amount, total, limit, skew):
    loads = [(1 << 20) // math.isqrt(standing ** skew) + 1 for standing in range(2, amount + 1)]
    spare, given = total - limit - (amount - 1), [1] * (amount - 1)
    while spare > 0:
        movable = [i for i in range(amount - 1) if given[i] < limit]
        whole, budget = sum([loads[i] for i in movable]), spare
        for i in movable:
            more = min(limit - given[i], max(1, budget * loads[i] // whole), spare)
            given[i] = given[i] + more
            spare = spare - more
    return np.array([limit] + given)


def ragged(key, count, total, most, skew):
    if count == 2:
        one = jax.random.randint(key, (), max(1, total - most), min(most, total - 1) + 1)
        return jnp.stack([one, total - one])
    sizes = jnp.asarray(length_profile(count, total, most, skew), jnp.int32)
    twos = (count - 1) // 2
    giver, sink = sizes[1:1 + 2 * twos:2], sizes[2:2 + 2 * twos:2]
    slack = jnp.minimum(giver - 1, most - sink)
    passed = jax.random.randint(jax.random.fold_in(key, 1), (twos,), 0, 1 << 20) % (slack + 1)
    sizes = sizes.at[1:1 + 2 * twos:2].set(giver - passed).at[2:2 + 2 * twos:2].set(sink + passed)
    return sizes[jax.random.permutation(jax.random.fold_in(key, 2), count)]


def scatter_about(rng, dims, deviation, reach, shards=(), kind=jnp.bfloat16):
    drawn = deviation * jax.random.normal(rng, dims, jnp.float32)
    if shards:
        drawn = drawn * level_of(rng, dims, shards, -0.22, 0.18)
    return jnp.clip(drawn, -reach, reach).astype(kind)


def setup_inputs(seed: int = 0) -> dict:
    arg_keys = jax.random.split(jax.random.key(seed), 10)
    inputs = scatter_about(arg_keys[0], (TOKENS, D), 1.0, 6.0, ((0, 8), (1, 4)))
    out_grads = scatter_about(arg_keys[1], (TOKENS, D), 1.0, 6.0, ((0, 8), (1, 4)))
    gate_pre = scatter_about(arg_keys[2], (TOKENS, FF), 1.0, 6.0, ((0, 8), (1, 4)))
    up_pre = scatter_about(arg_keys[3], (TOKENS, FF), 1.0, 6.0, ((0, 8), (1, 4)))
    hidden_grad = scatter_about(arg_keys[4], (TOKENS, FF), 1.0, 6.0, ((0, 8), (1, 4)))
    proj_model = scatter_about(arg_keys[5], (D, 2 * RANK), D ** -0.5, 0.0625, ((0, 32),))
    proj_hidden = scatter_about(arg_keys[6], (FF, 3 * RANK), FF ** -0.5, 0.03125, ((0, 32),))
    lengths = jax.vmap(lambda own: ragged(own, N_TENSOR, TOK_DEV, MOST, 2))(jax.random.split(arg_keys[7], N_DP)).reshape((N_DP, N_TENSOR)).astype(jnp.int32)
    owners = jax.vmap(lambda own: jax.random.permutation(own, N_TENSOR))(jax.random.split(arg_keys[8], N_DP)).reshape((N_DP, N_TENSOR)).astype(jnp.int32)
    return {"inputs": inputs, "out_grads": out_grads, "gate_pre": gate_pre, "up_pre": up_pre, "hidden_grad": hidden_grad, "proj_model": proj_model, "proj_hidden": proj_hidden, "lengths": lengths, "owners": owners}


def one_group(group, proj_model, proj_hidden):
    inputs, out_grads, gate_pre, up_pre, hidden_grad, lens, owner_row = group
    gate_value = gate_pre.astype(jnp.float32)
    up_value = up_pre.astype(jnp.float32)
    grad_value = hidden_grad.astype(jnp.float32)
    sigmoid_gate = jax.nn.sigmoid(gate_value)
    hidden = (gate_value * sigmoid_gate * up_value).astype(jnp.bfloat16)
    up_grad = (grad_value * gate_value * sigmoid_gate).astype(jnp.bfloat16)
    gate_grad = (grad_value * up_value * sigmoid_gate * (1.0 + gate_value * (1.0 - sigmoid_gate))).astype(jnp.bfloat16)
    gate_out = jnp.dot(gate_grad, proj_hidden[:, :RANK], preferred_element_type=jnp.float32)
    up_out = jnp.dot(up_grad, proj_hidden[:, RANK:2 * RANK], preferred_element_type=jnp.float32)
    hidden_in = jnp.dot(hidden, proj_hidden[:, 2 * RANK:], preferred_element_type=jnp.float32)
    model_in = jnp.dot(inputs, proj_model[:, :RANK], preferred_element_type=jnp.float32)
    model_out = jnp.dot(out_grads, proj_model[:, RANK:], preferred_element_type=jnp.float32)
    starts = (jnp.cumsum(lens) - lens).astype(jnp.int32)
    places = jnp.arange(TOK_DEV, dtype=jnp.int32)
    masks = ((places[None, :] >= starts[:, None]) & (places[None, :] < (starts + lens)[:, None])).astype(jnp.float32)
    pairs = ((gate_out, model_in), (up_out, model_in), (model_out, hidden_in))
    blocks = [jnp.einsum("et,ta,tb->eab", masks, left_side, right_side, precision=lax.Precision.HIGHEST) for left_side, right_side in pairs]
    feats = jnp.stack(blocks, axis=1).reshape(N_TENSOR, FEAT)
    return jnp.zeros_like(feats).at[owner_row].set(feats)


def reference(inputs, out_grads, gate_pre, up_pre, hidden_grad, proj_model, proj_hidden, lengths, owners):
    grouped = (
        inputs.reshape(N_DP, TOK_DEV, D),
        out_grads.reshape(N_DP, TOK_DEV, D),
        gate_pre.reshape(N_DP, TOK_DEV, FF),
        up_pre.reshape(N_DP, TOK_DEV, FF),
        hidden_grad.reshape(N_DP, TOK_DEV, FF),
        lengths,
        owners,
    )
    result = lax.map(lambda group: one_group(group, proj_model, proj_hidden), grouped)
    return result.reshape(EXAMPLES, FEAT)
```

```python
import functools
import math

import jax
import jax.numpy as jnp
from jax import lax
from jax.experimental import pallas as pl
from jax.experimental.pallas import tpu as pltpu
from jax.sharding import PartitionSpec as P

MESH = pl.DeviceIdType.MESH
NT = (((1,), (1,)), ((), ()))
TN = (((0,), (0,)), ((), ()))
F32 = jnp.float32
BF16 = jnp.bfloat16
ROWS = 32
ALONG = 2
PIECES = ((128, 64), (0, 64), (64, 64))


def kernel(
    nz, nx, ny,
    inp_h, og_h, gp_h, up_h, hg_h, pm_h, wt_h, lens, owns,
    out,
    raw, act, inp_v, og_v, pmb, wtb, acc, part, rx1, chip, sx2, rx2, full, fs,
    raw_sem, io_sem, own_sem, recv, s_up, s_dn, s_x, r_sem, t_sem, r2_sem, t2_sem,
):
    ndp = nz * nx
    me = lax.axis_index("dp")
    t = lax.axis_index("tensor")
    z, x = me // nx, me % nx
    y, c = t // 2, t % 2
    mate = y * 2 + 1 - c
    units = wt_h.shape[1]
    feats = pm_h.shape[0]
    toks = inp_h.shape[0]
    half = toks // 2
    sources = (gp_h, up_h, hg_h)

    def raw_copy(block, slot, q):
        cols = pl.ds(pl.multiple_of(block * units, 128), units)
        return pltpu.make_async_copy(sources[q].at[:, cols], raw.at[slot, q], raw_sem.at[slot, q])

    for q in range(3):
        raw_copy(0, 0, q).start()
    io = (pltpu.make_async_copy(inp_h, inp_v, io_sem.at[0]),
          pltpu.make_async_copy(og_h, og_v, io_sem.at[1]))
    pieces = 1 + len(PIECES)
    own = [pm_h] + [wt_h.at[pl.ds(row, n), :] for row, n in PIECES]

    def held(p, slot):
        return pmb.at[slot] if p == 0 else wtb.at[slot, pl.ds(*PIECES[p - 1]), :]

    barrier = pltpu.get_barrier_semaphore()

    def greet(d, s):
        pl.semaphore_signal(barrier, inc=1, device_id=(d, s), device_id_type=MESH)

    for j in range(1, nx):
        greet(z * nx + (x + j) % nx, t)
    for j in range(1, ny):
        greet(me, ((y + j) % ny) * 2 + c)
    greet(me, mate)

    @pl.when(z < nz - 1)
    def _():
        greet(me + nx, t)

    @pl.when(z > 0)
    def _():
        greet(me - nx, t)

    pl.semaphore_wait(
        barrier, nx + ny - 1 + (z < nz - 1).astype(jnp.int32) + (z > 0).astype(jnp.int32)
    )

    def remote(p, src, slot, sem, d):
        return pltpu.make_async_remote_copy(
            src_ref=src, dst_ref=held(p, slot), send_sem=sem, recv_sem=recv.at[slot, p],
            device_id=(d, t), device_id_type=MESH,
        )

    def across(p, src, slot, j):
        return remote(p, src, slot, s_x.at[slot, p, j - 1], z * nx + (x + j) % nx)

    def upward(p, src, slot):
        return remote(p, src, slot, s_up.at[slot, p], me + nx)

    def downward(p, src, slot):
        return remote(p, src, slot, s_dn.at[slot, p], me - nx)

    for p in range(pieces):
        @pl.when(z < nz - 1)
        def _():
            upward(p, own[p], me).start()

        @pl.when(z > 0)
        def _():
            downward(p, own[p], me).start()

        for j in range(1, nx):
            across(p, own[p], me, j).start()
    keep = [pltpu.make_async_copy(own[p], held(p, me), own_sem.at[p]) for p in range(pieces)]
    for p in range(pieces):
        keep[p].start()
    for copy in io:
        copy.start()
    acc[...] = jnp.zeros_like(acc)

    def elementwise(block, carry):
        slot = block % 2

        @pl.when(block + 1 < ndp)
        def _():
            for q in range(3):
                raw_copy(block + 1, 1 - slot, q).start()

        for q in range(3):
            raw_copy(block, slot, q).wait()

        def some(i, carry):
            rows = pl.ds(pl.multiple_of(i * ROWS, ROWS), ROWS)
            gate = raw[slot, 0, rows, :].astype(F32)
            up = raw[slot, 1, rows, :].astype(F32)
            grad = raw[slot, 2, rows, :].astype(F32)
            sig = 0.5 * jnp.tanh(0.5 * gate) + 0.5
            silu = gate * sig
            act[0, block, rows, :] = (grad * up * (sig + silu * (1.0 - sig))).astype(BF16)
            act[1, block, rows, :] = (grad * silu).astype(BF16)
            act[2, block, rows, :] = (silu * up).astype(BF16)
            return carry

        lax.fori_loop(0, toks // ROWS, some, 0)
        return carry

    lax.fori_loop(0, ndp, elementwise, 0)
    for copy in io:
        copy.wait()
    for p in range(pieces):
        keep[p].wait()

    def dots(slot):
        cols = pl.ds(pl.multiple_of(slot * feats, 128), feats)
        weights = pmb[slot]
        pair = wtb[slot, pl.ds(0, 128), :]
        acc[0] += lax.dot_general(act[0, slot], pair, NT, preferred_element_type=F32)
        acc[1] += lax.dot_general(act[1, slot], pair, NT, preferred_element_type=F32)
        acc[2] += jnp.dot(inp_v[:, cols], weights, preferred_element_type=F32)
        acc[3] += jnp.dot(og_v[:, cols], weights, preferred_element_type=F32)
        acc[4, :, pl.ds(0, 64)] += lax.dot_general(
            act[2, slot], wtb[slot, pl.ds(128, 64), :], NT, preferred_element_type=F32
        )

    def along(p, src_z):
        low_end = (src_z == 0) & ((z == 1) | (z == nz - 1))
        high_end = (src_z == nz - 1) & ((z == nz - 2) | (z == 0))
        return low_end | high_end if p < ALONG else src_z < 0

    def passes_up(p, src_z):
        return (src_z == 0) & ((z == 0) | (z == nz - 2)) if p < ALONG else src_z < 0

    def passes_down(p, src_z):
        return (src_z == nz - 1) & ((z == nz - 1) | (z == 1)) if p < ALONG else src_z < 0

    near = jnp.minimum(z, nz - 1 - z)

    def plane(i):
        k = (i + 1) // 2
        paired = jnp.where(i % 2 == 1, z + k, z - k)
        far = jnp.where(z < nz - 1 - z, z + i - near, z - i + near)
        return jnp.where(i <= 2 * near, paired, far)

    def step(i, carry):
        @pl.when(i < nz)
        def _():
            src_z = plane(i)
            slot = src_z * nx + x

            @pl.when(i > 0)
            def _():
                for p in range(pieces):
                    block = held(p, slot)
                    across(p, block, slot, 1).wait_recv()

                    @pl.when((src_z < z) & (z < nz - 1))
                    def _():
                        upward(p, block, slot).start()

                    @pl.when((src_z > z) & (z > 0))
                    def _():
                        downward(p, block, slot).start()

                    @pl.when(jnp.logical_not(along(p, src_z)))
                    def _():
                        for j in range(1, nx):
                            across(p, block, slot, j).start()

            dots(slot)

        @pl.when(i > 0)
        def _():
            src_z = plane(i - 1)
            for j in range(1, nx):
                slot = src_z * nx + (x + j) % nx
                for p in range(pieces):
                    block = held(p, slot)
                    across(p, block, slot, 1).wait_recv()

                    @pl.when(passes_up(p, src_z))
                    def _():
                        upward(p, block, slot).start()

                    @pl.when(passes_down(p, src_z))
                    def _():
                        downward(p, block, slot).start()

                dots(slot)

        return carry

    lax.fori_loop(0, nz + 1, step, 0)

    low = lax.broadcasted_iota(jnp.int32, (toks, 128), 1) < 64
    part[0] = jnp.where(low, acc[0], acc[1])
    part[1] = jnp.where(low, acc[2], acc[3])
    part[2] = acc[4]
    mine = pl.ds(pl.multiple_of(c * half, half), half)
    other = pl.ds(pl.multiple_of((1 - c) * half, half), half)
    first = [
        pltpu.make_async_remote_copy(
            src_ref=part.at[k, other, :], dst_ref=rx1.at[k], send_sem=t_sem.at[0, k],
            recv_sem=r_sem.at[0, k], device_id=(me, mate), device_id_type=MESH,
        )
        for k in range(3)
    ]
    swaps = [
        [
            pltpu.make_async_remote_copy(
                src_ref=sx2.at[k], dst_ref=rx2.at[j - 1, k], send_sem=t2_sem.at[j - 1, k],
                recv_sem=r2_sem.at[j - 1, k],
                device_id=(me, ((y + j) % ny) * 2 + c), device_id_type=MESH,
            )
            for j in range(1, ny)
        ]
        for k in range(3)
    ]
    last = [
        pltpu.make_async_remote_copy(
            src_ref=full.at[c, k], dst_ref=full.at[c, k], send_sem=t_sem.at[1, k],
            recv_sem=r_sem.at[1, k], device_id=(me, mate), device_id_type=MESH,
        )
        for k in range(3)
    ]
    for copy in first:
        copy.start()
    for k in range(3):
        first[k].wait_recv()
        both = part[k, mine, :] + rx1[k]
        chip[k] = both
        sx2[k] = both.astype(BF16)
        for copy in swaps[k]:
            copy.start()
    for k in range(3):
        whole = chip[k]
        for j in range(1, ny):
            swaps[k][j - 1].wait_recv()
            whole = whole + rx2[j - 1, k].astype(F32)
        full[c, k] = whole
        last[k].start()

    start, length, seen = jnp.int32(0), jnp.int32(0), jnp.int32(0)
    for e in range(2 * ny):
        hit = owns[0, e] == t
        start = jnp.where(hit, seen, start)
        length = jnp.where(hit, lens[0, e], length)
        seen = seen + lens[0, e]
    for copy in last:
        copy.wait_recv()

    places = lax.broadcasted_iota(jnp.int32, (half, 128), 0)
    pair_one = jnp.zeros((128, 128), F32)
    pair_two = jnp.zeros((128, 128), F32)
    for h in range(2):
        token = places + h * half
        inside = (token >= start) & (token < start + length)
        model = full[h, 1]
        pair_one += lax.dot_general(
            jnp.where(inside, full[h, 0], 0.0), model, TN,
            precision=lax.Precision.HIGHEST, preferred_element_type=F32,
        )
        pair_two += lax.dot_general(
            jnp.where(inside, model, 0.0), full[h, 2], TN,
            precision=lax.Precision.HIGHEST, preferred_element_type=F32,
        )
    fs[pl.ds(0, 128), :] = pair_one
    fs[pl.ds(128, 64), :] = pair_two[64:, :]
    even = fs[pl.ds(0, 96, stride=2), :]
    odd = fs[pl.ds(1, 96, stride=2), :]
    out[...] = jnp.concatenate([even[:, :64], odd[:, :64]], axis=1)

    for k in range(3):
        first[k].wait_send()
        last[k].wait_send()
        for copy in swaps[k]:
            copy.wait_send()

    def drain(src_z, carry):
        slot = src_z * nx + x
        for p in range(pieces):
            block = held(p, slot)

            @pl.when((src_z <= z) & (z < nz - 1))
            def _():
                upward(p, block, slot).wait_send()

            @pl.when((src_z >= z) & (z > 0))
            def _():
                downward(p, block, slot).wait_send()

            @pl.when(jnp.logical_not(along(p, src_z)))
            def _():
                for j in range(1, nx):
                    across(p, block, slot, j).wait_send()

            for j in range(1, nx):
                slot_b = src_z * nx + (x + j) % nx
                block_b = held(p, slot_b)

                @pl.when(passes_up(p, src_z))
                def _():
                    upward(p, block_b, slot_b).wait_send()

                @pl.when(passes_down(p, src_z))
                def _():
                    downward(p, block_b, slot_b).wait_send()
        return carry

    lax.fori_loop(0, nz, drain, 0)


def fused(
    nz, nx, ny,
    inputs, out_grads, gate_pre, up_pre, hidden_grad, proj_model, proj_hidden, lengths, owners,
):
    ndp = nz * nx
    toks, wide = inputs.shape
    units, feats = proj_hidden.shape[0], proj_model.shape[0]
    half = toks // 2
    hbm = pl.BlockSpec(memory_space=pltpu.HBM)
    smem = pl.BlockSpec(memory_space=pltpu.SMEM)
    dma = pltpu.SemaphoreType.DMA
    out = pl.pallas_call(
        functools.partial(kernel, nz, nx, ny),
        out_shape=pltpu.VMEM((96, 128), F32),
        in_specs=[hbm] * 7 + [smem] * 2,
        out_specs=pl.BlockSpec(memory_space=pltpu.VMEM),
        scratch_shapes=[
            pltpu.VMEM((2, 3, toks, units), BF16),
            pltpu.VMEM((3, ndp, toks, units), BF16),
            pltpu.VMEM((toks, wide), BF16),
            pltpu.VMEM((toks, wide), BF16),
            pltpu.VMEM((ndp, feats, 128), BF16),
            pltpu.VMEM((ndp, 192, units), BF16),
            pltpu.VMEM((5, toks, 128), F32),
            pltpu.VMEM((3, toks, 128), F32),
            pltpu.VMEM((3, half, 128), F32),
            pltpu.VMEM((3, half, 128), F32),
            pltpu.VMEM((3, half, 128), BF16),
            pltpu.VMEM((ny - 1, 3, half, 128), BF16),
            pltpu.VMEM((2, 3, half, 128), F32),
            pltpu.VMEM((192, 128), F32),
            dma((2, 3)),
            dma((2,)),
            dma((1 + len(PIECES),)),
            dma((ndp, 1 + len(PIECES))),
            dma((ndp, 1 + len(PIECES))),
            dma((ndp, 1 + len(PIECES))),
            dma((ndp, 1 + len(PIECES), nx - 1)),
            dma((2, 3)),
            dma((2, 3)),
            dma((ny - 1, 3)),
            dma((ny - 1, 3)),
        ],
        compiler_params=pltpu.CompilerParams(
            collective_id=0, has_side_effects=True, vmem_limit_bytes=60416 << 10
        ),
    )(inputs, out_grads, gate_pre, up_pre, hidden_grad, proj_model, proj_hidden.T, lengths, owners)
    return out.reshape(1, 3 * 64 * 64)


def per_device(
    inputs, out_grads, gate_pre, up_pre, hidden_grad, proj_model, proj_hidden, lengths, owners
):
    rank_width = proj_model.shape[1] // 2
    tok_rows = inputs.shape[0]
    gate_value = gate_pre.astype(jnp.float32)
    up_value = up_pre.astype(jnp.float32)
    grad_value = hidden_grad.astype(jnp.float32)
    sigmoid_gate = jax.nn.sigmoid(gate_value)
    hidden = (gate_value * sigmoid_gate * up_value).astype(jnp.bfloat16)
    up_grad = (grad_value * gate_value * sigmoid_gate).astype(jnp.bfloat16)
    gate_grad = (
        grad_value * up_value * sigmoid_gate * (1.0 + gate_value * (1.0 - sigmoid_gate))
    ).astype(jnp.bfloat16)
    sources = (gate_grad, up_grad, hidden)
    block_rows = lax.all_gather(proj_hidden, "dp", axis=0, tiled=True)
    parts = []
    for column, source in enumerate(sources):
        parts.append(
            jnp.dot(
                source,
                block_rows[:, column * rank_width : (column + 1) * rank_width],
                preferred_element_type=jnp.float32,
            )
        )
    hidden_part = jnp.concatenate(parts, axis=1)
    block_rows = lax.all_gather(proj_model, "dp", axis=0, tiled=True)
    first_part = jnp.dot(inputs, block_rows[:, :rank_width], preferred_element_type=jnp.float32)
    second_part = jnp.dot(out_grads, block_rows[:, rank_width:], preferred_element_type=jnp.float32)
    model_part = jnp.concatenate([first_part, second_part], axis=1)
    partial_value = jnp.concatenate([hidden_part, model_part], axis=1)
    lens = lengths[0]
    owner_row = owners[0]
    order = jnp.arange(lens.shape[0], dtype=jnp.int32)
    starts = jnp.sum(jnp.where(order[None, :] < order[:, None], lens[None, :], 0), axis=1)
    myself = lax.axis_index("tensor")
    tensor_count = lax.axis_size("tensor")
    chosen = (owner_row == myself).astype(jnp.int32)
    my_length = jnp.sum(lens * chosen)
    capacity = 3 * tok_rows // tensor_count
    slots = jnp.arange(capacity * lax.axis_size("tensor"), dtype=jnp.int32)
    holder = slots // capacity
    within = slots % capacity
    matched = (owner_row[None, :] == holder[:, None]).astype(jnp.int32)
    first_token = jnp.sum(matched * starts[None, :], axis=1)
    span = jnp.sum(matched * lens[None, :], axis=1)
    valid = within < span
    picked = jnp.where(valid, first_token + within, 0)
    summed = lax.psum_scatter(
        jnp.take(partial_value, picked, axis=0) * valid[:, None].astype(jnp.float32),
        "tensor",
        scatter_dimension=0,
        tiled=True,
    )
    weights = (jnp.arange(capacity, dtype=jnp.int32) < my_length).astype(jnp.float32)

    def block_of(index):
        return summed[:, index * rank_width : (index + 1) * rank_width]

    pairs = ((0, 3), (1, 3), (4, 2))
    blocks = []
    for left_index, right_index in pairs:
        left_side = block_of(left_index) * weights[:, None]
        blocks.append(
            jnp.einsum(
                "ta,tb->ab", left_side, block_of(right_index), precision=lax.Precision.HIGHEST
            )
        )
    return jnp.stack(blocks, axis=0).reshape(1, 3 * rank_width * rank_width)


def solution(mesh):
    in_specs = (
        P("dp", "tensor"),
        P("dp", "tensor"),
        P("dp", "tensor"),
        P("dp", "tensor"),
        P("dp", "tensor"),
        P(("tensor", "dp"), None),
        P(("tensor", "dp"), None),
        P("dp", None),
        P("dp", None),
    )
    out_specs = P(("dp", "tensor"), None)
    ndp, ny = mesh.shape["dp"], mesh.shape["tensor"] // 2

    def program(*args):
        units, feats, rank_width = args[6].shape[0], args[5].shape[0], args[5].shape[1] // 2
        nx = math.isqrt(ndp // 2)
        fits = units % 128 == 0 and feats % 128 == 0 and rank_width == 64
        if fits and ny > 1 and nx > 1 and ndp // nx > 3 and ndp % nx == 0 and args[0].shape[0] % 64 == 0:
            return fused(ndp // nx, nx, ny, *args)
        return per_device(*args)

    return jax.shard_map(
        program, mesh=mesh, in_specs=in_specs, out_specs=out_specs, check_vma=False
    )
```

```python
import functools
import math

import jax
import jax.numpy as jnp
from jax import lax
from jax.experimental import pallas as pl
from jax.experimental.pallas import tpu as pltpu
from jax.sharding import PartitionSpec as P

MESH = pl.DeviceIdType.MESH
NT = (((1,), (1,)), ((), ()))
F32 = jnp.float32
BF16 = jnp.bfloat16
ROWS = 32
PM, HID, UP, GATE = range(4)
END = (
    (0, 0, PM), (0, 0, HID), (0, 0, UP), (0, 0, GATE),
    (1, 0, PM), (0, 1, PM), (1, 0, HID), (0, 1, HID),
    (0, 1, UP), (1, 0, UP), (2, 0, PM), (1, 1, PM),
    (0, 1, GATE), (1, 0, GATE), (2, 0, HID), (1, 1, HID),
    (2, 1, PM), (2, 0, UP), (3, 0, PM), (2, 1, HID),
    (2, 0, GATE), (2, 1, UP), (3, 1, PM), (3, 0, HID),
    (2, 1, GATE), (3, 0, UP), (3, 1, HID), (3, 0, GATE),
    (3, 1, UP), (1, 1, UP), (3, 1, GATE), (1, 1, GATE),
)
MID = (
    (1, 0, PM), (1, 0, HID), (1, 0, UP), (1, 0, GATE),
    (0, 0, PM), (2, 0, PM), (1, 1, PM), (2, 0, HID),
    (0, 0, HID), (1, 1, HID), (2, 0, UP), (0, 0, UP),
    (1, 1, UP), (3, 0, PM), (0, 1, PM), (0, 0, GATE),
    (2, 1, PM), (2, 0, GATE), (0, 1, HID), (1, 1, GATE),
    (3, 0, HID), (3, 1, PM), (0, 1, UP), (3, 0, UP),
    (2, 1, HID), (0, 1, GATE), (3, 0, GATE), (2, 1, UP),
    (2, 1, GATE), (3, 1, HID), (3, 1, UP), (3, 1, GATE),
)
MODEL_SENT, MODEL_SUMMED = 22, 27
HID_DONE = (27, 29)
UP_DONE = (29, 30)
PER = 6


def packed(events):
    words = []
    for at in range(0, len(events), PER):
        word = 0
        for j, (plane, other, piece) in enumerate(events[at : at + PER]):
            word += ((plane + 4 * other) * 4 + piece) << (5 * j)
        words.append(word)
    return words


def kernel(
    nz, nx, ny,
    inp_h, og_h, gp_h, up_h, hg_h, pm_h, wt_h, lens, owns,
    out,
    raw, act, inp_v, og_v, pmb, wtb, macc, wacc, mtx, mtxb, mrx, mrxb, mm, fs, fh, ftx, frx,
    raw_sem, io_sem, own_sem, recv, s_in, s_out, s_x, mt_sem, mr_sem, ft_sem, fr_sem,
):
    ndp = nz * nx
    nt = 2 * ny
    me = lax.axis_index("dp")
    t = lax.axis_index("tensor")
    z, x = me // nx, me % nx
    low_half = z < nz // 2
    r = jnp.where(low_half, z, nz - 1 - z)
    inward = me + jnp.where(low_half, nx, -nx)
    outward = me - jnp.where(low_half, nx, -nx)
    across = z * nx + 1 - x
    end = r == 0
    units = wt_h.shape[1]
    feats = pm_h.shape[0]
    toks = inp_h.shape[0]
    sources = (gp_h, up_h, hg_h)

    def raw_copy(block, slot, q):
        cols = pl.ds(pl.multiple_of(block * units, 128), units)
        return pltpu.make_async_copy(sources[q].at[:, cols], raw.at[slot, q], raw_sem.at[slot, q])

    for q in range(3):
        raw_copy(0, 0, q).start()
    io = (pltpu.make_async_copy(inp_h, inp_v, io_sem.at[0]),
          pltpu.make_async_copy(og_h, og_v, io_sem.at[1]))
    own = [pm_h] + [wt_h.at[pl.ds(64 * (3 - p), 64), :] for p in (HID, UP, GATE)]

    barrier = pltpu.get_barrier_semaphore()

    def greet(d, s):
        pl.semaphore_signal(barrier, inc=1, device_id=(d, s), device_id_type=MESH)

    greet(across, t)
    greet(inward, t)

    @pl.when(jnp.logical_not(end))
    def _():
        greet(outward, t)

    for j in range(1, nt):
        greet(me, (t + j) % nt)
    pl.semaphore_wait(barrier, nt + 1 + r)

    def held(p, slot):
        return pmb.at[slot] if p is PM else wtb.at[slot, p - 1]

    def remote(src, dst, slot, p, sems, d):
        return pltpu.make_async_remote_copy(
            src_ref=src, dst_ref=dst, send_sem=sems.at[slot, p], recv_sem=recv.at[slot, p],
            device_id=(d, t), device_id_type=MESH,
        )

    def routes(src, dst, slot, p):
        return (remote(src, dst, slot, p, s_in, inward),
                remote(src, dst, slot, p, s_out, outward),
                remote(src, dst, slot, p, s_x, across))

    def wanted(q, other, p):
        same = jnp.logical_not(other)
        mine = same & (q == r)
        mid = jnp.logical_not(end)
        go_in = mine | (mid & same & (q == 0)) | (end & other & (q == 0) & (p > 0))
        go_out = mid & (mine | (same & (q >= 2)) | (other & (q == 1) & (p >= 2)))
        go_x = same & (
            mine
            | (end & jnp.logical_not((q == 1) & (p >= 2)))
            | (mid & ((q >= 2) | (p == 0)))
        )
        return go_in, go_out, go_x

    def slot_of(q, other):
        return jnp.where(low_half, q, nz - 1 - q) * nx + jnp.where(other, 1 - x, x)

    def begin(copies, conditions):
        for copy, condition in zip(copies, conditions):
            @pl.when(condition)
            def _():
                copy.start()

    def send_own(p):
        begin(routes(own[p], held(p, me), me, p), (r >= 0, jnp.logical_not(end), r >= 0))

    for p in (PM, HID, UP):
        send_own(p)
    keep = [pltpu.make_async_copy(own[p], held(p, me), own_sem.at[p]) for p in range(4)]
    for p in range(4):
        keep[p].start()
    for copy in io:
        copy.start()
    macc[...] = jnp.zeros_like(macc)
    wacc[...] = jnp.zeros_like(wacc)

    def near(q):
        slot = slot_of(q, False)
        copies = routes(pmb.at[slot], pmb.at[slot], slot, PM)
        copies[2].wait_recv()
        begin(copies, wanted(jnp.int32(q), False, PM))

    def elementwise(block, carry):
        slot = block % 2

        @pl.when(block + 1 < ndp)
        def _():
            for q in range(3):
                raw_copy(block + 1, 1 - slot, q).start()

        @pl.when(block == ndp // 2)
        def _():
            @pl.when(end)
            def _():
                near(1)

            @pl.when(jnp.logical_not(end))
            def _():
                near(0)
                near(2)

            send_own(GATE)

        for q in range(3):
            raw_copy(block, slot, q).wait()

        def some(i, carry):
            rows = pl.ds(pl.multiple_of(i * ROWS, ROWS), ROWS)
            gate = raw[slot, 0, rows, :].astype(F32)
            up = raw[slot, 1, rows, :].astype(F32)
            grad = raw[slot, 2, rows, :].astype(F32)
            sig = 0.5 * jnp.tanh(0.5 * gate) + 0.5
            silu = gate * sig
            act[0, block, rows, :] = (silu * up).astype(BF16)
            act[1, block, rows, :] = (grad * silu).astype(BF16)
            act[2, block, rows, :] = (grad * up * (sig + silu * (1.0 - sig))).astype(BF16)
            return carry

        lax.fori_loop(0, toks // ROWS, some, 0)
        return carry

    lax.fori_loop(0, ndp, elementwise, 0)
    for copy in io:
        copy.wait()
    for p in range(4):
        keep[p].wait()

    first_lanes = lax.broadcasted_iota(jnp.int32, (toks, 128), 1) < 64
    first = lax.broadcasted_iota(jnp.int32, (32, 128), 1) < 64

    c = t % 2
    y = t // 2
    mate_copy = pltpu.make_async_remote_copy(
        src_ref=mtx, dst_ref=mrx, send_sem=mt_sem.at[0], recv_sem=mr_sem.at[0],
        device_id=(me, y * 2 + 1 - c), device_id_type=MESH,
    )
    far_copies = [
        pltpu.make_async_remote_copy(
            src_ref=mtxb, dst_ref=mrxb.at[j], send_sem=mt_sem.at[1 + j], recv_sem=mr_sem.at[1 + j],
            device_id=(me, (1 - y) * 2 + (c + j) % 2), device_id_type=MESH,
        )
        for j in range(2)
    ]

    def send_model():
        both = jnp.where(first_lanes, macc[0], macc[1])
        mtx[...] = both
        mtxb[...] = both.astype(BF16)
        for copy in far_copies:
            copy.start()
        mate_copy.start()

    def sum_model():
        mate_copy.wait_recv()
        for copy in far_copies:
            copy.wait_recv()
        full = mtx[...] + mrx[...] + (mrxb[0].astype(F32) + mrxb[1].astype(F32))
        turned = pltpu.roll(full, 64, 1)
        pair = (jnp.where(first_lanes, full, turned), jnp.where(first_lanes, turned, full))
        starts, stops = [], []
        for s in range(nt):
            start, stop, seen = jnp.int32(0), jnp.int32(0), jnp.int32(0)
            for e in range(nt):
                hit = owns[0, e] == s
                start = jnp.where(hit, seen, start)
                seen = seen + lens[0, e]
                stop = jnp.where(hit, seen, stop)
            starts.append(start)
            stops.append(stop)
        token = lax.broadcasted_iota(jnp.int32, (toks, 128), 0)
        for h in range(nt // 2):
            start = jnp.where(first_lanes, starts[2 * h], starts[2 * h + 1])
            stop = jnp.where(first_lanes, stops[2 * h], stops[2 * h + 1])
            inside = (token >= start) & (token < stop)
            for side in range(2):
                value = jnp.where(inside, pair[side], 0.0)
                high = value.astype(BF16)
                mm[side, 0, :, pl.ds(128 * h, 128)] = high
                mm[side, 1, :, pl.ds(128 * h, 128)] = (value - high.astype(F32)).astype(BF16)

    def products(k, side):
        value = wacc[k]
        high = value.astype(BF16)
        rest = (value - high.astype(F32)).astype(BF16)

        def dot(left, right):
            return jnp.dot(left, right, preferred_element_type=F32)

        return dot(high, mm[side, 0]) + (dot(high, mm[side, 1]) + dot(rest, mm[side, 0]))

    def feature_copy(k, j):
        s = (t + j) % nt
        return pltpu.make_async_remote_copy(
            src_ref=ftx.at[k, s], dst_ref=frx.at[k, j - 1], send_sem=ft_sem.at[k, j - 1],
            recv_sem=fr_sem.at[k, j - 1], device_id=(me, s), device_id_type=MESH,
        )

    def send_features(k):
        for j in range(1, nt):
            feature_copy(k, j).start()

    def features_in(k):
        value = products(k, 0)
        for h in range(nt // 2):
            fs[h] = value[:, 128 * h : 128 * h + 128]
            even = fs[h, pl.ds(0, 32, stride=2), :]
            odd = fs[h, pl.ds(1, 32, stride=2), :]
            ftx[k, 2 * h] = jnp.where(first, even, pltpu.roll(odd, 64, 1))
            ftx[k, 2 * h + 1] = jnp.where(first, pltpu.roll(even, 64, 1), odd)
        send_features(k)

    def features_out():
        fh[:, pl.ds(0, 64)] = products(0, 1).T
        for s in range(nt):
            even = fh[pl.ds(64 * s, 32, stride=2), :]
            odd = fh[pl.ds(64 * s + 1, 32, stride=2), :]
            ftx[0, s] = jnp.concatenate([even[:, :64], odd[:, :64]], axis=1)
        send_features(0)

    words = [jnp.where(end, jnp.int32(a), jnp.int32(b)) for a, b in zip(packed(END), packed(MID))]

    def decode(i):
        word = words[0]
        for j in range(1, len(words)):
            word = jnp.where(i // PER == j, words[j], word)
        code = lax.shift_right_logical(word, 5 * (i % PER)) % 32
        return (code // 4) % 4, code // 16 == 1, code % 4

    def event(i, carry):
        q, other, p = decode(i)
        slot = slot_of(q, other)
        mine = jnp.logical_not(other) & (q == r)
        beside = (q - r == 1) | (r - q == 1)
        done = mine | ((p == 0) & jnp.logical_not(other) & beside)
        todo = jnp.logical_not(done)
        go_in, go_out, go_x = wanted(q, other, p)
        go = (todo & go_in, todo & go_out & jnp.logical_not(other), todo & go_x)

        @pl.when(p == 0)
        def _():
            copies = routes(pmb.at[slot], pmb.at[slot], slot, PM)

            @pl.when(todo)
            def _():
                copies[2].wait_recv()

            begin(copies, go)
            cols = pl.ds(pl.multiple_of(slot * feats, 128), feats)
            weights = pmb[slot]
            macc[0] += jnp.dot(inp_v[:, cols], weights, preferred_element_type=F32)
            macc[1] += jnp.dot(og_v[:, cols], weights, preferred_element_type=F32)

        @pl.when(p > 0)
        def _():
            ref = wtb.at[slot, p - 1]
            copies = routes(ref, ref, slot, p)

            @pl.when(todo)
            def _():
                copies[2].wait_recv()

            begin(copies, go)

            @pl.when(jnp.logical_not(end) & jnp.logical_not(other) & (q == nz - 1) & (p == GATE))
            def _():
                for late in (UP, GATE):
                    block = wtb.at[across, late - 1]
                    remote(block, block, across, late, s_out, outward).start()

            wacc[p - 1] += lax.dot_general(
                wtb[slot, p - 1], act[p - 1, slot], NT, preferred_element_type=F32
            )

        @pl.when(i == MODEL_SENT)
        def _():
            send_model()

        @pl.when(i == MODEL_SUMMED)
        def _():
            sum_model()

        @pl.when(i == jnp.where(end, HID_DONE[0], HID_DONE[1]))
        def _():
            features_out()

        at_up = i == jnp.where(end, UP_DONE[0], UP_DONE[1])

        @pl.when(at_up | (i == len(END) - 1))
        def _():
            features_in(jnp.where(at_up, 1, 2))

        return carry

    lax.fori_loop(0, len(END), event, 0)

    def drain(i, carry):
        q, other, p = decode(i)
        slot = slot_of(q, other)
        go = wanted(q, other, p)

        def finish(copies):
            for copy, condition in zip(copies, go):
                @pl.when(condition)
                def _():
                    copy.wait_send()

        @pl.when(p == 0)
        def _():
            finish(routes(pmb.at[slot], pmb.at[slot], slot, PM))

        @pl.when(p > 0)
        def _():
            finish(routes(wtb.at[slot, p - 1], wtb.at[slot, p - 1], slot, p))

        return carry

    lax.fori_loop(0, len(END), drain, 0)
    mate_copy.wait_send()
    for copy in far_copies:
        copy.wait_send()
    for k in range(3):
        total = ftx[k, t]
        for j in range(1, nt):
            feature_copy(k, j).wait_recv()
            total = total + frx[k, j - 1]
        out[pl.ds(32 * (2, 1, 0)[k], 32), :] = total
    for k in range(3):
        for j in range(1, nt):
            feature_copy(k, j).wait_send()


def fused(
    nz, nx, ny,
    inputs, out_grads, gate_pre, up_pre, hidden_grad, proj_model, proj_hidden, lengths, owners,
):
    ndp = nz * nx
    nt = 2 * ny
    toks, wide = inputs.shape
    units, feats = proj_hidden.shape[0], proj_model.shape[0]
    hbm = pl.BlockSpec(memory_space=pltpu.HBM)
    smem = pl.BlockSpec(memory_space=pltpu.SMEM)
    dma = pltpu.SemaphoreType.DMA
    out = pl.pallas_call(
        functools.partial(kernel, nz, nx, ny),
        out_shape=pltpu.VMEM((96, 128), F32),
        in_specs=[hbm] * 7 + [smem] * 2,
        out_specs=pl.BlockSpec(memory_space=pltpu.VMEM),
        scratch_shapes=[
            pltpu.VMEM((2, 3, toks, units), BF16),
            pltpu.VMEM((3, ndp, toks, units), BF16),
            pltpu.VMEM((toks, wide), BF16),
            pltpu.VMEM((toks, wide), BF16),
            pltpu.VMEM((ndp, feats, 128), BF16),
            pltpu.VMEM((ndp, 3, 64, units), BF16),
            pltpu.VMEM((2, toks, 128), F32),
            pltpu.VMEM((3, 64, toks), F32),
            pltpu.VMEM((toks, 128), F32),
            pltpu.VMEM((toks, 128), BF16),
            pltpu.VMEM((toks, 128), F32),
            pltpu.VMEM((2, toks, 128), BF16),
            pltpu.VMEM((2, 2, toks, 64 * nt), BF16),
            pltpu.VMEM((nt // 2, 64, 128), F32),
            pltpu.VMEM((64 * nt, 128), F32),
            pltpu.VMEM((3, nt, 32, 128), F32),
            pltpu.VMEM((3, nt - 1, 32, 128), F32),
            dma((2, 3)),
            dma((2,)),
            dma((4,)),
            dma((ndp, 4)),
            dma((ndp, 4)),
            dma((ndp, 4)),
            dma((ndp, 4)),
            dma((3,)),
            dma((3,)),
            dma((3, nt - 1)),
            dma((3, nt - 1)),
        ],
        compiler_params=pltpu.CompilerParams(
            collective_id=0, has_side_effects=True, vmem_limit_bytes=60416 << 10
        ),
    )(inputs, out_grads, gate_pre, up_pre, hidden_grad, proj_model, proj_hidden.T, lengths, owners)
    return out.reshape(1, 3 * 64 * 64)


def per_device(
    inputs, out_grads, gate_pre, up_pre, hidden_grad, proj_model, proj_hidden, lengths, owners
):
    rank_width = proj_model.shape[1] // 2
    tok_rows = inputs.shape[0]
    gate_value = gate_pre.astype(jnp.float32)
    up_value = up_pre.astype(jnp.float32)
    grad_value = hidden_grad.astype(jnp.float32)
    sigmoid_gate = jax.nn.sigmoid(gate_value)
    hidden = (gate_value * sigmoid_gate * up_value).astype(jnp.bfloat16)
    up_grad = (grad_value * gate_value * sigmoid_gate).astype(jnp.bfloat16)
    gate_grad = (
        grad_value * up_value * sigmoid_gate * (1.0 + gate_value * (1.0 - sigmoid_gate))
    ).astype(jnp.bfloat16)
    sources = (gate_grad, up_grad, hidden)
    block_rows = lax.all_gather(proj_hidden, "dp", axis=0, tiled=True)
    parts = []
    for column, source in enumerate(sources):
        parts.append(
            jnp.dot(
                source,
                block_rows[:, column * rank_width : (column + 1) * rank_width],
                preferred_element_type=jnp.float32,
            )
        )
    hidden_part = jnp.concatenate(parts, axis=1)
    block_rows = lax.all_gather(proj_model, "dp", axis=0, tiled=True)
    first_part = jnp.dot(inputs, block_rows[:, :rank_width], preferred_element_type=jnp.float32)
    second_part = jnp.dot(out_grads, block_rows[:, rank_width:], preferred_element_type=jnp.float32)
    model_part = jnp.concatenate([first_part, second_part], axis=1)
    partial_value = jnp.concatenate([hidden_part, model_part], axis=1)
    lens = lengths[0]
    owner_row = owners[0]
    order = jnp.arange(lens.shape[0], dtype=jnp.int32)
    starts = jnp.sum(jnp.where(order[None, :] < order[:, None], lens[None, :], 0), axis=1)
    myself = lax.axis_index("tensor")
    tensor_count = lax.axis_size("tensor")
    chosen = (owner_row == myself).astype(jnp.int32)
    my_length = jnp.sum(lens * chosen)
    capacity = 3 * tok_rows // tensor_count
    slots = jnp.arange(capacity * lax.axis_size("tensor"), dtype=jnp.int32)
    holder = slots // capacity
    within = slots % capacity
    matched = (owner_row[None, :] == holder[:, None]).astype(jnp.int32)
    first_token = jnp.sum(matched * starts[None, :], axis=1)
    span = jnp.sum(matched * lens[None, :], axis=1)
    valid = within < span
    picked = jnp.where(valid, first_token + within, 0)
    summed = lax.psum_scatter(
        jnp.take(partial_value, picked, axis=0) * valid[:, None].astype(jnp.float32),
        "tensor",
        scatter_dimension=0,
        tiled=True,
    )
    weights = (jnp.arange(capacity, dtype=jnp.int32) < my_length).astype(jnp.float32)

    def block_of(index):
        return summed[:, index * rank_width : (index + 1) * rank_width]

    pairs = ((0, 3), (1, 3), (4, 2))
    blocks = []
    for left_index, right_index in pairs:
        left_side = block_of(left_index) * weights[:, None]
        blocks.append(
            jnp.einsum(
                "ta,tb->ab", left_side, block_of(right_index), precision=lax.Precision.HIGHEST
            )
        )
    return jnp.stack(blocks, axis=0).reshape(1, 3 * rank_width * rank_width)


def solution(mesh):
    in_specs = (
        P("dp", "tensor"),
        P("dp", "tensor"),
        P("dp", "tensor"),
        P("dp", "tensor"),
        P("dp", "tensor"),
        P(("tensor", "dp"), None),
        P(("tensor", "dp"), None),
        P("dp", None),
        P("dp", None),
    )
    out_specs = P(("dp", "tensor"), None)
    ndp, ny = mesh.shape["dp"], mesh.shape["tensor"] // 2

    def program(*args):
        units, feats, rank_width = args[6].shape[0], args[5].shape[0], args[5].shape[1] // 2
        nx = math.isqrt(ndp // 2)
        fits = units % 128 == 0 and feats % 128 == 0 and rank_width == 64 and args[0].shape[0] % 128 == 0
        if fits and (nx, ny) == (2, 2) and ndp == 4 * nx:
            return fused(ndp // nx, nx, ny, *args)
        return per_device(*args)

    return jax.shard_map(
        program, mesh=mesh, in_specs=in_specs, out_specs=out_specs, check_vma=False
    )
```

```python
import functools
import math

import jax
import jax.numpy as jnp
from jax import lax
from jax.experimental import pallas as pl
from jax.experimental.pallas import tpu as pltpu
from jax.sharding import PartitionSpec as P

MESH = pl.DeviceIdType.MESH
NT = (((1,), (1,)), ((), ()))
F32 = jnp.float32
BF16 = jnp.bfloat16
ROWS = 32
PM, HID, UP, GATE = range(4)
END = (
    (0, 0, PM), (0, 0, HID), (0, 0, UP), (0, 0, GATE),
    (1, 0, PM), (1, 0, HID), (0, 1, PM), (0, 1, HID),
    (1, 0, UP), (0, 1, UP), (2, 0, PM), (1, 1, PM),
    (2, 0, HID), (0, 1, GATE), (1, 1, HID), (2, 0, UP),
    (2, 1, PM), (3, 0, PM), (2, 1, HID), (2, 0, GATE),
    (2, 1, UP), (3, 0, HID), (3, 1, PM), (3, 0, UP),
    (2, 1, GATE), (3, 0, GATE), (3, 1, HID), (1, 1, UP),
    (3, 1, UP), (1, 0, GATE), (3, 1, GATE), (1, 1, GATE),
)
MID = (
    (1, 0, PM), (1, 0, HID), (1, 0, UP), (1, 0, GATE),
    (0, 0, PM), (2, 0, PM), (2, 0, HID), (0, 0, HID),
    (1, 1, PM), (1, 1, HID), (2, 0, UP), (0, 0, UP),
    (1, 1, UP), (3, 0, PM), (0, 1, PM), (0, 0, GATE),
    (2, 1, PM), (2, 0, GATE), (0, 1, HID), (1, 1, GATE),
    (3, 0, HID), (0, 1, UP), (2, 1, HID), (3, 0, UP),
    (0, 1, GATE), (2, 1, UP), (3, 0, GATE), (3, 1, PM),
    (2, 1, GATE), (3, 1, HID), (3, 1, UP), (3, 1, GATE),
)
MODEL_SENT = (22, 27)
MODEL_SUMMED = (26, 29)
HID_DONE = (26, 29)
UP_DONE = (28, 30)
SPLIT = 16
PER = 6


def packed(events):
    words = []
    for at in range(0, len(events), PER):
        word = 0
        for j, (plane, other, piece) in enumerate(events[at : at + PER]):
            word += ((plane + 4 * other) * 4 + piece) << (5 * j)
        words.append(word)
    return words


def kernel(
    nz, nx, ny,
    inp_h, og_h, gp_h, up_h, hg_h, pm_h, wt_h, lens, owns,
    out,
    raw, act, io_v, pmb, wtb, macc, wacc, mtx, mtxb, mrx, mrxb, mm, fs, fh, ftx, frx,
    raw_sem, io_sem, own_sem, recv, w_sem, p_sem, mt_sem, mr_sem, ft_sem, fr_sem,
):
    ndp = nz * nx
    nt = 2 * ny
    me = lax.axis_index("dp")
    t = lax.axis_index("tensor")
    z, x = me // nx, me % nx
    low_half = z < nz // 2
    r = jnp.where(low_half, z, nz - 1 - z)
    inward = me + jnp.where(low_half, nx, -nx)
    outward = me - jnp.where(low_half, nx, -nx)
    across = z * nx + 1 - x
    end = r == 0
    units = wt_h.shape[1]
    feats = pm_h.shape[0]
    toks = inp_h.shape[0]
    sources = (gp_h, up_h, hg_h)

    def raw_copy(block, slot, q):
        cols = pl.ds(pl.multiple_of(block * units, 128), units)
        return pltpu.make_async_copy(sources[q].at[:, cols], raw.at[slot, q], raw_sem.at[slot])

    for q in range(3):
        raw_copy(0, 0, q).start()
    io = (pltpu.make_async_copy(inp_h, io_v.at[0], io_sem.at[0]),
          pltpu.make_async_copy(og_h, io_v.at[1], io_sem.at[0]))

    barrier = pltpu.get_barrier_semaphore()

    def greet(d, s):
        pl.semaphore_signal(barrier, inc=1, device_id=(d, s), device_id_type=MESH)

    greet(across, t)
    greet(inward, t)

    @pl.when(jnp.logical_not(end))
    def _():
        greet(outward, t)

    for j in range(1, nt):
        greet(me, (t + j) % nt)
    pl.semaphore_wait(barrier, nt + 1 + r)

    def rows_of(slot, p, first=0, count=64):
        return wtb.at[pl.ds(pl.multiple_of(slot * 192 + (3 - p) * 64 + first, 16), count), :]

    def remote(src, dst, slot, p, sem, d):
        return pltpu.make_async_remote_copy(
            src_ref=src, dst_ref=dst, send_sem=sem, recv_sem=recv.at[slot, p],
            device_id=(d, t), device_id_type=MESH,
        )

    def routes(src, dst, slot, p, sems):
        return tuple(
            remote(src, dst, slot, p, sems.at[k], d) for k, d in enumerate((inward, outward, across))
        )

    def model_routes(slot):
        return routes(pmb.at[slot], pmb.at[slot], slot, PM, p_sem)

    def hidden_routes(slot, p):
        return routes(rows_of(slot, p), rows_of(slot, p), slot, p, w_sem)

    def wanted(q, other, p):
        same = jnp.logical_not(other)
        mid = jnp.logical_not(end)
        go_in = (mid & same & (q == 0)) | (end & other & (q == 0) & (p > 0))
        go_out = mid & same & (q >= 2)
        go_x = same & ((end & ((q >= 2) | (p <= HID))) | (mid & ((q >= 2) | (p == 0))))
        return go_in, go_out, go_x

    def slot_of(q, other):
        return jnp.where(low_half, q, nz - 1 - q) * nx + jnp.where(other, 1 - x, x)

    def begin(copies, conditions):
        for copy, condition in zip(copies, conditions):
            @pl.when(condition)
            def _():
                copy.start()

    def send_own(p):
        if p is PM:
            copies = routes(pm_h, pmb.at[me], me, PM, p_sem)
        else:
            own = wt_h.at[pl.ds((3 - p) * 64, 64), :]
            copies = routes(own, rows_of(me, p), me, p, w_sem)
        copies[0].start()
        if p is not GATE:
            @pl.when(jnp.logical_not(end))
            def _():
                copies[1].start()
        copies[2].start()

    for p in (PM, HID, UP):
        send_own(p)
    keep = (
        pltpu.make_async_copy(pm_h, pmb.at[me], own_sem.at[0]),
        pltpu.make_async_copy(wt_h, wtb.at[pl.ds(pl.multiple_of(me * 192, 64), 192), :], own_sem.at[1]),
    )
    for copy in keep:
        copy.start()
    for copy in io:
        copy.start()
    macc[...] = jnp.zeros_like(macc)
    wacc[...] = jnp.zeros_like(wacc)

    def near(q, p):
        slot = slot_of(q, False)
        copies = model_routes(slot) if p is PM else hidden_routes(slot, p)
        copies[2].wait_recv()
        begin(copies, wanted(jnp.int32(q), False, p))

    def elementwise(block, carry):
        slot = block % 2

        @pl.when(block + 1 < ndp)
        def _():
            for q in range(3):
                raw_copy(block + 1, 1 - slot, q).start()

        for at, p in ((ndp // 2, PM), (3 * ndp // 4, HID)):
            @pl.when((block == at) & end)
            def _():
                near(1, p)

            @pl.when((block == at) & jnp.logical_not(end))
            def _():
                near(2, p)
                near(0, p)

        @pl.when(block == ndp // 2)
        def _():
            send_own(GATE)

        pltpu.make_async_copy(raw.at[slot], raw.at[slot], raw_sem.at[slot]).wait()

        def some(i, carry):
            rows = pl.ds(pl.multiple_of(i * ROWS, ROWS), ROWS)
            gate = raw[slot, 0, rows, :].astype(F32)
            up = raw[slot, 1, rows, :].astype(F32)
            grad = raw[slot, 2, rows, :].astype(F32)
            sig = 0.5 * jnp.tanh(0.5 * gate) + 0.5
            silu = gate * sig
            act[0, block, rows, :] = (silu * up).astype(BF16)
            act[1, block, rows, :] = (grad * silu).astype(BF16)
            act[2, block, rows, :] = (grad * up * (sig + silu * (1.0 - sig))).astype(BF16)
            return carry

        lax.fori_loop(0, toks // ROWS, some, 0)
        return carry

    lax.fori_loop(0, ndp, elementwise, 0)
    pltpu.make_async_copy(io_v, io_v, io_sem.at[0]).wait()
    for copy in keep:
        copy.wait()

    first_lanes = lax.broadcasted_iota(jnp.int32, (toks, 128), 1) < 64
    first = lax.broadcasted_iota(jnp.int32, (32, 128), 1) < 64

    c = t % 2
    y = t // 2
    mate_copy = pltpu.make_async_remote_copy(
        src_ref=mtx, dst_ref=mrx, send_sem=mt_sem.at[0], recv_sem=mr_sem.at[0],
        device_id=(me, y * 2 + 1 - c), device_id_type=MESH,
    )
    far_copies = [
        pltpu.make_async_remote_copy(
            src_ref=mtxb, dst_ref=mrxb.at[j], send_sem=mt_sem.at[1], recv_sem=mr_sem.at[1],
            device_id=(me, (1 - y) * 2 + (c + j) % 2), device_id_type=MESH,
        )
        for j in range(2)
    ]
    far_both = pltpu.make_async_remote_copy(
        src_ref=mrxb, dst_ref=mrxb, send_sem=mt_sem.at[1], recv_sem=mr_sem.at[1],
        device_id=(me, (1 - y) * 2 + c), device_id_type=MESH,
    )

    def send_model():
        both = jnp.where(first_lanes, macc[0], macc[1])
        mtx[...] = both
        mtxb[...] = both.astype(BF16)
        for copy in far_copies:
            copy.start()
        mate_copy.start()

    def sum_model():
        mate_copy.wait_recv()
        far_both.wait_recv()
        full = mtx[...] + mrx[...] + (mrxb[0].astype(F32) + mrxb[1].astype(F32))
        turned = pltpu.roll(full, 64, 1)
        pair = (jnp.where(first_lanes, full, turned), jnp.where(first_lanes, turned, full))
        starts, stops = [], []
        for s in range(nt):
            start, stop, seen = jnp.int32(0), jnp.int32(0), jnp.int32(0)
            for e in range(nt):
                hit = owns[0, e] == s
                start = jnp.where(hit, seen, start)
                seen = seen + lens[0, e]
                stop = jnp.where(hit, seen, stop)
            starts.append(start)
            stops.append(stop)
        token = lax.broadcasted_iota(jnp.int32, (toks, 128), 0)
        for h in range(nt // 2):
            start = jnp.where(first_lanes, starts[2 * h], starts[2 * h + 1])
            stop = jnp.where(first_lanes, stops[2 * h], stops[2 * h + 1])
            inside = (token >= start) & (token < stop)
            for side in range(2):
                value = jnp.where(inside, pair[side], 0.0)
                high = value.astype(BF16)
                mm[side, 0, :, pl.ds(128 * h, 128)] = high
                mm[side, 1, :, pl.ds(128 * h, 128)] = (value - high.astype(F32)).astype(BF16)

    def products(k, side):
        value = wacc[k]
        high = value.astype(BF16)
        rest = (value - high.astype(F32)).astype(BF16)

        def dot(left, right):
            return jnp.dot(left, right, preferred_element_type=F32)

        return dot(high, mm[side, 0]) + (dot(high, mm[side, 1]) + dot(rest, mm[side, 0]))

    def feature_copy(k, j):
        s = (t + j) % nt
        return pltpu.make_async_remote_copy(
            src_ref=ftx.at[k, s], dst_ref=frx.at[k, j - 1], send_sem=ft_sem.at[0],
            recv_sem=fr_sem.at[k], device_id=(me, s), device_id_type=MESH,
        )

    def feature_wait(ref, k):
        return pltpu.make_async_remote_copy(
            src_ref=ref, dst_ref=ref, send_sem=ft_sem.at[0], recv_sem=fr_sem.at[k],
            device_id=(me, (t + 1) % nt), device_id_type=MESH,
        )

    def send_features(k):
        for j in range(1, nt):
            feature_copy(k, j).start()

    def features_in(k):
        value = products(k, 0)
        for h in range(nt // 2):
            fs[h] = value[:, 128 * h : 128 * h + 128]
            even = fs[h, pl.ds(0, 32, stride=2), :]
            odd = fs[h, pl.ds(1, 32, stride=2), :]
            ftx[k, 2 * h] = jnp.where(first, even, pltpu.roll(odd, 64, 1))
            ftx[k, 2 * h + 1] = jnp.where(first, pltpu.roll(even, 64, 1), odd)
        send_features(k)

    def features_out():
        fh[:, pl.ds(0, 64)] = products(0, 1).T
        for s in range(nt):
            even = fh[pl.ds(64 * s, 32, stride=2), :]
            odd = fh[pl.ds(64 * s + 1, 32, stride=2), :]
            ftx[0, s] = jnp.concatenate([even[:, :64], odd[:, :64]], axis=1)
        send_features(0)

    words = [jnp.where(end, jnp.int32(a), jnp.int32(b)) for a, b in zip(packed(END), packed(MID))]

    def decode(i):
        word = words[0]
        for j in range(1, len(words)):
            word = jnp.where(i // PER == j, words[j], word)
        code = lax.shift_right_logical(word, 5 * (i % PER)) % 32
        return (code // 4) % 4, code // 16 == 1, code % 4

    def event(i, carry):
        q, other, p = decode(i)
        slot = slot_of(q, other)
        mine = jnp.logical_not(other) & (q == r)
        beside = (q - r == 1) | (r - q == 1)
        todo = jnp.logical_not(mine | ((p <= HID) & jnp.logical_not(other) & beside))
        go = tuple(todo & g for g in wanted(q, other, p))

        @pl.when(p == 0)
        def _():
            copies = model_routes(slot)

            @pl.when(todo)
            def _():
                copies[2].wait_recv()

            begin(copies, go)
            cols = pl.ds(pl.multiple_of(slot * feats, 128), feats)
            weights = pmb[slot]
            macc[0] += jnp.dot(io_v[0, :, cols], weights, preferred_element_type=F32)
            macc[1] += jnp.dot(io_v[1, :, cols], weights, preferred_element_type=F32)

        @pl.when(p > 0)
        def _():
            copies = hidden_routes(slot, p)

            @pl.when(todo)
            def _():
                copies[2].wait_recv()

            begin(copies, go)

            @pl.when(end & jnp.logical_not(other) & (q == 1) & (p == UP))
            def _():
                part = rows_of(slot, UP, 0, SPLIT)
                remote(part, part, slot, UP, w_sem.at[2], across).start()

            @pl.when(jnp.logical_not(end) & jnp.logical_not(other) & (q == nz - 1) & (p == GATE))
            def _():
                for late, of, start in ((UP, across, SPLIT), (GATE, me, 0), (GATE, across, 0)):
                    part = rows_of(of, late, start, 64 - start)
                    remote(part, part, of, late, w_sem.at[1], outward).start()

            wacc[p - 1] += lax.dot_general(
                rows_of(slot, p)[...], act[p - 1, slot], NT, preferred_element_type=F32
            )

        @pl.when(i == jnp.where(end, MODEL_SENT[0], MODEL_SENT[1]))
        def _():
            send_model()

        @pl.when(i == jnp.where(end, MODEL_SUMMED[0], MODEL_SUMMED[1]))
        def _():
            sum_model()

        @pl.when(i == jnp.where(end, HID_DONE[0], HID_DONE[1]))
        def _():
            features_out()

        at_up = i == jnp.where(end, UP_DONE[0], UP_DONE[1])

        @pl.when(at_up | (i == len(END) - 1))
        def _():
            features_in(jnp.where(at_up, 1, 2))

        return carry

    lax.fori_loop(0, len(END), event, 0)

    def all_sent(ref, sem):
        pltpu.make_async_remote_copy(
            src_ref=ref, dst_ref=ref, send_sem=sem, recv_sem=recv.at[me, PM],
            device_id=(across, t), device_id_type=MESH,
        ).wait_send()

    def sent(k, blocks, rows):
        all_sent(pmb.at[pl.ds(0, blocks)], p_sem.at[k])
        all_sent(wtb.at[pl.ds(0, rows), :], w_sem.at[k])

    @pl.when(end)
    def _():
        sent(0, 1, 384)
        sent(2, 4, 640 + SPLIT)

    @pl.when(jnp.logical_not(end))
    def _():
        sent(0, 2, 384)
        sent(1, 3, 704 - SPLIT)
        sent(2, 4, 576)

    mate_copy.wait_send()
    far_both.wait_send()
    for k in range(3):
        total = ftx[k, t]
        feature_wait(frx.at[k], k).wait_recv()
        for j in range(1, nt):
            total = total + frx[k, j - 1]
        out[pl.ds(32 * (2, 1, 0)[k], 32), :] = total
    feature_wait(frx, 0).wait_send()


def fused(
    nz, nx, ny,
    inputs, out_grads, gate_pre, up_pre, hidden_grad, proj_model, proj_hidden, lengths, owners,
):
    ndp = nz * nx
    nt = 2 * ny
    toks, wide = inputs.shape
    units, feats = proj_hidden.shape[0], proj_model.shape[0]
    hbm = pl.BlockSpec(memory_space=pltpu.HBM)
    smem = pl.BlockSpec(memory_space=pltpu.SMEM)
    dma = pltpu.SemaphoreType.DMA
    out = pl.pallas_call(
        functools.partial(kernel, nz, nx, ny),
        out_shape=pltpu.VMEM((96, 128), F32),
        in_specs=[hbm] * 7 + [smem] * 2,
        out_specs=pl.BlockSpec(memory_space=pltpu.VMEM),
        scratch_shapes=[
            pltpu.VMEM((2, 3, toks, units), BF16),
            pltpu.VMEM((3, ndp, toks, units), BF16),
            pltpu.VMEM((2, toks, wide), BF16),
            pltpu.VMEM((ndp, feats, 128), BF16),
            pltpu.VMEM((ndp * 192, units), BF16),
            pltpu.VMEM((2, toks, 128), F32),
            pltpu.VMEM((3, 64, toks), F32),
            pltpu.VMEM((toks, 128), F32),
            pltpu.VMEM((toks, 128), BF16),
            pltpu.VMEM((toks, 128), F32),
            pltpu.VMEM((2, toks, 128), BF16),
            pltpu.VMEM((2, 2, toks, 64 * nt), BF16),
            pltpu.VMEM((nt // 2, 64, 128), F32),
            pltpu.VMEM((64 * nt, 128), F32),
            pltpu.VMEM((3, nt, 32, 128), F32),
            pltpu.VMEM((3, nt - 1, 32, 128), F32),
            dma((2,)),
            dma((1,)),
            dma((2,)),
            dma((ndp, 4)),
            dma((3,)),
            dma((3,)),
            dma((2,)),
            dma((2,)),
            dma((1,)),
            dma((3,)),
        ],
        compiler_params=pltpu.CompilerParams(
            collective_id=0, has_side_effects=True, vmem_limit_bytes=60416 << 10
        ),
    )(inputs, out_grads, gate_pre, up_pre, hidden_grad, proj_model, proj_hidden.T, lengths, owners)
    return out.reshape(1, 3 * 64 * 64)


def per_device(
    inputs, out_grads, gate_pre, up_pre, hidden_grad, proj_model, proj_hidden, lengths, owners
):
    rank_width = proj_model.shape[1] // 2
    tok_rows = inputs.shape[0]
    gate_value = gate_pre.astype(jnp.float32)
    up_value = up_pre.astype(jnp.float32)
    grad_value = hidden_grad.astype(jnp.float32)
    sigmoid_gate = jax.nn.sigmoid(gate_value)
    hidden = (gate_value * sigmoid_gate * up_value).astype(jnp.bfloat16)
    up_grad = (grad_value * gate_value * sigmoid_gate).astype(jnp.bfloat16)
    gate_grad = (
        grad_value * up_value * sigmoid_gate * (1.0 + gate_value * (1.0 - sigmoid_gate))
    ).astype(jnp.bfloat16)
    sources = (gate_grad, up_grad, hidden)
    block_rows = lax.all_gather(proj_hidden, "dp", axis=0, tiled=True)
    parts = []
    for column, source in enumerate(sources):
        parts.append(
            jnp.dot(
                source,
                block_rows[:, column * rank_width : (column + 1) * rank_width],
                preferred_element_type=jnp.float32,
            )
        )
    hidden_part = jnp.concatenate(parts, axis=1)
    block_rows = lax.all_gather(proj_model, "dp", axis=0, tiled=True)
    first_part = jnp.dot(inputs, block_rows[:, :rank_width], preferred_element_type=jnp.float32)
    second_part = jnp.dot(out_grads, block_rows[:, rank_width:], preferred_element_type=jnp.float32)
    model_part = jnp.concatenate([first_part, second_part], axis=1)
    partial_value = jnp.concatenate([hidden_part, model_part], axis=1)
    lens = lengths[0]
    owner_row = owners[0]
    order = jnp.arange(lens.shape[0], dtype=jnp.int32)
    starts = jnp.sum(jnp.where(order[None, :] < order[:, None], lens[None, :], 0), axis=1)
    myself = lax.axis_index("tensor")
    tensor_count = lax.axis_size("tensor")
    chosen = (owner_row == myself).astype(jnp.int32)
    my_length = jnp.sum(lens * chosen)
    capacity = 3 * tok_rows // tensor_count
    slots = jnp.arange(capacity * lax.axis_size("tensor"), dtype=jnp.int32)
    holder = slots // capacity
    within = slots % capacity
    matched = (owner_row[None, :] == holder[:, None]).astype(jnp.int32)
    first_token = jnp.sum(matched * starts[None, :], axis=1)
    span = jnp.sum(matched * lens[None, :], axis=1)
    valid = within < span
    picked = jnp.where(valid, first_token + within, 0)
    summed = lax.psum_scatter(
        jnp.take(partial_value, picked, axis=0) * valid[:, None].astype(jnp.float32),
        "tensor",
        scatter_dimension=0,
        tiled=True,
    )
    weights = (jnp.arange(capacity, dtype=jnp.int32) < my_length).astype(jnp.float32)

    def block_of(index):
        return summed[:, index * rank_width : (index + 1) * rank_width]

    pairs = ((0, 3), (1, 3), (4, 2))
    blocks = []
    for left_index, right_index in pairs:
        left_side = block_of(left_index) * weights[:, None]
        blocks.append(
            jnp.einsum(
                "ta,tb->ab", left_side, block_of(right_index), precision=lax.Precision.HIGHEST
            )
        )
    return jnp.stack(blocks, axis=0).reshape(1, 3 * rank_width * rank_width)


def solution(mesh):
    in_specs = (
        P("dp", "tensor"),
        P("dp", "tensor"),
        P("dp", "tensor"),
        P("dp", "tensor"),
        P("dp", "tensor"),
        P(("tensor", "dp"), None),
        P(("tensor", "dp"), None),
        P("dp", None),
        P("dp", None),
    )
    out_specs = P(("dp", "tensor"), None)
    ndp, ny = mesh.shape["dp"], mesh.shape["tensor"] // 2

    def program(*args):
        units, feats, rank_width = args[6].shape[0], args[5].shape[0], args[5].shape[1] // 2
        nx = math.isqrt(ndp // 2)
        fits = units % 128 == 0 and feats % 128 == 0 and rank_width == 64 and args[0].shape[0] % 128 == 0
        if fits and (nx, ny) == (2, 2) and ndp == 4 * nx:
            return fused(ndp // nx, nx, ny, *args)
        return per_device(*args)

    return jax.shard_map(
        program, mesh=mesh, in_specs=in_specs, out_specs=out_specs, check_vma=False
    )
```

```python
import functools
import math

import jax
import jax.numpy as jnp
from jax import lax
from jax.experimental import pallas as pl
from jax.experimental.pallas import tpu as pltpu
from jax.sharding import PartitionSpec as P

MESH = pl.DeviceIdType.MESH
NT = (((1,), (1,)), ((), ()))
F32 = jnp.float32
BF16 = jnp.bfloat16
ROWS = 32
PM, HID, UP, GATE = range(4)
END = (
    (0, 0, PM), (0, 0, HID), (0, 0, UP), (0, 0, GATE),
    (1, 0, PM), (1, 0, HID), (0, 1, PM), (0, 1, HID),
    (1, 0, UP), (0, 1, UP), (2, 0, PM), (1, 1, PM),
    (2, 0, HID), (0, 1, GATE), (1, 1, HID), (2, 0, UP),
    (2, 1, PM), (3, 0, PM), (2, 1, HID), (2, 0, GATE),
    (2, 1, UP), (3, 0, HID), (3, 1, PM), (3, 0, UP),
    (2, 1, GATE), (3, 0, GATE), (3, 1, HID), (1, 1, UP),
    (3, 1, UP), (1, 0, GATE), (3, 1, GATE), (1, 1, GATE),
)
MID = (
    (1, 0, PM), (1, 0, HID), (1, 0, UP), (1, 0, GATE),
    (0, 0, PM), (2, 0, PM), (2, 0, HID), (0, 0, HID),
    (1, 1, PM), (1, 1, HID), (2, 0, UP), (0, 0, UP),
    (1, 1, UP), (3, 0, PM), (0, 1, PM), (0, 0, GATE),
    (2, 1, PM), (2, 0, GATE), (0, 1, HID), (1, 1, GATE),
    (3, 0, HID), (0, 1, UP), (2, 1, HID), (3, 0, UP),
    (0, 1, GATE), (2, 1, UP), (3, 0, GATE), (3, 1, PM),
    (2, 1, GATE), (3, 1, HID), (3, 1, UP), (3, 1, GATE),
)
MODEL_SENT = (22, 27)
MODEL_SUMMED = (26, 29)
HID_DONE = (26, 29)
UP_DONE = (28, 30)
SPLIT = 32
PER = 6


def packed(events):
    words = []
    for at in range(0, len(events), PER):
        word = 0
        for j, (plane, other, piece) in enumerate(events[at : at + PER]):
            word += ((plane + 4 * other) * 4 + piece) << (5 * j)
        words.append(word)
    return words


def kernel(
    nz, nx, ny,
    inp_h, og_h, gp_h, up_h, hg_h, pm_h, wt_h, lens_h, owns_h,
    out,
    raw, act, io_v, pmb, wtb, macc, wacc, mtx, mtxb, mrx, mrxb, mm, fs, fh, ftx, frx, lens, owns,
    raw_sem, io_sem, own_sem, recv, w_sem, p_sem, mt_sem, mr_sem, ft_sem, fr_sem,
):
    ndp = nz * nx
    nt = 2 * ny
    me = lax.axis_index("dp")
    t = lax.axis_index("tensor")
    z, x = me // nx, me % nx
    low_half = z < nz // 2
    r = jnp.where(low_half, z, nz - 1 - z)
    inward = me + jnp.where(low_half, nx, -nx)
    outward = me - jnp.where(low_half, nx, -nx)
    across = z * nx + 1 - x
    end = r == 0
    units = wt_h.shape[1]
    feats = pm_h.shape[0]
    toks = inp_h.shape[0]
    sources = (gp_h, up_h, hg_h)

    def raw_copy(block, q):
        cols = pl.ds(block * units, units)
        return pltpu.make_async_copy(sources[q].at[:, cols], raw.at[block, q], raw_sem.at[block])

    io = (pltpu.make_async_copy(inp_h, io_v.at[0], io_sem.at[0]),
          pltpu.make_async_copy(og_h, io_v.at[1], io_sem.at[0]))

    barrier = pltpu.get_barrier_semaphore()

    def greet(d, s):
        pl.semaphore_signal(barrier, inc=1, device_id=(d, s), device_id_type=MESH)

    greet(across, t)
    greet(inward, t)

    @pl.when(jnp.logical_not(end))
    def _():
        greet(outward, t)

    for j in range(1, nt):
        greet(me, (t + j) % nt)
    for block in range(ndp):
        for q in range(3):
            raw_copy(block, q).start()
    pl.semaphore_wait(barrier, nt + 1 + r)

    def rows_of(slot, p, first=0, count=64):
        return wtb.at[pl.ds(pl.multiple_of(slot * 192 + (3 - p) * 64 + first, 16), count), :]

    def remote(src, dst, slot, p, sem, d):
        return pltpu.make_async_remote_copy(
            src_ref=src, dst_ref=dst, send_sem=sem, recv_sem=recv.at[slot, p],
            device_id=(d, t), device_id_type=MESH,
        )

    def routes(src, dst, slot, p, sems):
        return tuple(
            remote(src, dst, slot, p, sems.at[k], d) for k, d in enumerate((inward, outward, across))
        )

    def model_routes(slot):
        return routes(pmb.at[slot], pmb.at[slot], slot, PM, p_sem)

    def hidden_routes(slot, p):
        return routes(rows_of(slot, p), rows_of(slot, p), slot, p, w_sem)

    def wanted(q, other, p):
        same = jnp.logical_not(other)
        mid = jnp.logical_not(end)
        go_in = (mid & same & (q == 0)) | (end & other & (q == 0) & (p > 0))
        go_out = mid & same & (q >= 2)
        go_x = same & ((end & ((q >= 2) | (p <= HID))) | (mid & ((q >= 2) | (p == 0))))
        return go_in, go_out, go_x

    def slot_of(q, other):
        return jnp.where(low_half, q, nz - 1 - q) * nx + jnp.where(other, 1 - x, x)

    def begin(copies, conditions):
        for copy, condition in zip(copies, conditions):
            @pl.when(condition)
            def _():
                copy.start()

    def send_own(p):
        if p is PM:
            copies = routes(pm_h, pmb.at[me], me, PM, p_sem)
        else:
            own = wt_h.at[pl.ds((3 - p) * 64, 64), :]
            copies = routes(own, rows_of(me, p), me, p, w_sem)
        copies[0].start()
        if p is not GATE:
            @pl.when(jnp.logical_not(end))
            def _():
                copies[1].start()
        copies[2].start()

    for p in (PM, HID, UP):
        send_own(p)
    keep = (
        pltpu.make_async_copy(pm_h, pmb.at[me], own_sem.at[0]),
        pltpu.make_async_copy(lens_h, lens, own_sem.at[2]),
        pltpu.make_async_copy(owns_h, owns, own_sem.at[3]),
        pltpu.make_async_copy(wt_h, wtb.at[pl.ds(pl.multiple_of(me * 192, 64), 192), :], own_sem.at[1]),
    )
    for copy in keep:
        copy.start()
    for copy in io:
        copy.start()
    macc[...] = jnp.zeros_like(macc)
    wacc[...] = jnp.zeros_like(wacc)

    def near(q, p):
        slot = slot_of(q, False)
        copies = model_routes(slot) if p is PM else hidden_routes(slot, p)
        copies[2].wait_recv()
        begin(copies, wanted(jnp.int32(q), False, p))

    def elementwise(block, carry):
        for at, p in ((ndp // 2, PM), (3 * ndp // 4, HID)):
            @pl.when((block == at) & end)
            def _():
                near(1, p)

            @pl.when((block == at) & jnp.logical_not(end))
            def _():
                near(2, p)
                near(0, p)

        @pl.when(block == ndp // 2)
        def _():
            send_own(GATE)

        pltpu.make_async_copy(raw.at[block], raw.at[block], raw_sem.at[block]).wait()

        def some(i, carry):
            rows = pl.ds(pl.multiple_of(i * ROWS, ROWS), ROWS)
            gate = raw[block, 0, rows, :].astype(F32)
            up = raw[block, 1, rows, :].astype(F32)
            grad = raw[block, 2, rows, :].astype(F32)
            sig = 0.5 * jnp.tanh(0.5 * gate) + 0.5
            silu = gate * sig
            act[0, block, rows, :] = (silu * up).astype(BF16)
            act[1, block, rows, :] = (grad * silu).astype(BF16)
            act[2, block, rows, :] = (grad * up * (sig + silu * (1.0 - sig))).astype(BF16)
            return carry

        lax.fori_loop(0, toks // ROWS, some, 0)
        return carry

    lax.fori_loop(0, ndp, elementwise, 0)
    pltpu.make_async_copy(io_v, io_v, io_sem.at[0]).wait()
    for copy in keep:
        copy.wait()

    first_lanes = lax.broadcasted_iota(jnp.int32, (toks, 128), 1) < 64
    first = lax.broadcasted_iota(jnp.int32, (32, 128), 1) < 64

    c = t % 2
    y = t // 2
    mate_copy = pltpu.make_async_remote_copy(
        src_ref=mtx, dst_ref=mrx, send_sem=mt_sem.at[0], recv_sem=mr_sem.at[0],
        device_id=(me, y * 2 + 1 - c), device_id_type=MESH,
    )
    far_copies = [
        pltpu.make_async_remote_copy(
            src_ref=mtxb, dst_ref=mrxb.at[j], send_sem=mt_sem.at[1], recv_sem=mr_sem.at[1],
            device_id=(me, (1 - y) * 2 + (c + j) % 2), device_id_type=MESH,
        )
        for j in range(2)
    ]
    far_both = pltpu.make_async_remote_copy(
        src_ref=mrxb, dst_ref=mrxb, send_sem=mt_sem.at[1], recv_sem=mr_sem.at[1],
        device_id=(me, (1 - y) * 2 + c), device_id_type=MESH,
    )

    def send_model():
        both = jnp.where(first_lanes, macc[0], macc[1])
        mtx[...] = both
        mtxb[...] = both.astype(BF16)
        for copy in far_copies:
            copy.start()
        mate_copy.start()

    def sum_model():
        mate_copy.wait_recv()
        far_both.wait_recv()
        full = mtx[...] + mrx[...] + (mrxb[0].astype(F32) + mrxb[1].astype(F32))
        turned = pltpu.roll(full, 64, 1)
        pair = (jnp.where(first_lanes, full, turned), jnp.where(first_lanes, turned, full))
        starts, stops = [], []
        for s in range(nt):
            start, stop, seen = jnp.int32(0), jnp.int32(0), jnp.int32(0)
            for e in range(nt):
                hit = owns[0, e] == s
                start = jnp.where(hit, seen, start)
                seen = seen + lens[0, e]
                stop = jnp.where(hit, seen, stop)
            starts.append(start)
            stops.append(stop)
        token = lax.broadcasted_iota(jnp.int32, (toks, 128), 0)
        for h in range(nt // 2):
            start = jnp.where(first_lanes, starts[2 * h], starts[2 * h + 1])
            stop = jnp.where(first_lanes, stops[2 * h], stops[2 * h + 1])
            inside = (token >= start) & (token < stop)
            for side in range(2):
                value = jnp.where(inside, pair[side], 0.0)
                high = value.astype(BF16)
                mm[side, 0, :, pl.ds(128 * h, 128)] = high
                mm[side, 1, :, pl.ds(128 * h, 128)] = (value - high.astype(F32)).astype(BF16)

    def products(k, side):
        value = wacc[k]
        high = value.astype(BF16)
        rest = (value - high.astype(F32)).astype(BF16)

        def dot(left, right):
            return jnp.dot(left, right, preferred_element_type=F32)

        return dot(high, mm[side, 0]) + (dot(high, mm[side, 1]) + dot(rest, mm[side, 0]))

    def feature_copy(k, j):
        s = (t + j) % nt
        return pltpu.make_async_remote_copy(
            src_ref=ftx.at[k, s], dst_ref=frx.at[k, j - 1], send_sem=ft_sem.at[0],
            recv_sem=fr_sem.at[k], device_id=(me, s), device_id_type=MESH,
        )

    def feature_wait(ref, k):
        return pltpu.make_async_remote_copy(
            src_ref=ref, dst_ref=ref, send_sem=ft_sem.at[0], recv_sem=fr_sem.at[k],
            device_id=(me, (t + 1) % nt), device_id_type=MESH,
        )

    def send_features(k):
        for j in range(1, nt):
            feature_copy(k, j).start()

    def features_in(k):
        value = products(k, 0)
        for h in range(nt // 2):
            fs[h] = value[:, 128 * h : 128 * h + 128]
            even = fs[h, pl.ds(0, 32, stride=2), :]
            odd = fs[h, pl.ds(1, 32, stride=2), :]
            ftx[k, 2 * h] = jnp.where(first, even, pltpu.roll(odd, 64, 1))
            ftx[k, 2 * h + 1] = jnp.where(first, pltpu.roll(even, 64, 1), odd)
        send_features(k)

    def features_out():
        fh[:, pl.ds(0, 64)] = products(0, 1).T
        for s in range(nt):
            even = fh[pl.ds(64 * s, 32, stride=2), :]
            odd = fh[pl.ds(64 * s + 1, 32, stride=2), :]
            ftx[0, s] = jnp.concatenate([even[:, :64], odd[:, :64]], axis=1)
        send_features(0)

    words = [jnp.where(end, jnp.int32(a), jnp.int32(b)) for a, b in zip(packed(END), packed(MID))]

    def decode(i):
        word = words[0]
        for j in range(1, len(words)):
            word = jnp.where(i // PER == j, words[j], word)
        code = lax.shift_right_logical(word, 5 * (i % PER)) % 32
        return (code // 4) % 4, code // 16 == 1, code % 4

    def event(i, carry):
        q, other, p = decode(i)
        slot = slot_of(q, other)
        mine = jnp.logical_not(other) & (q == r)
        beside = (q - r == 1) | (r - q == 1)
        todo = jnp.logical_not(mine | ((p <= HID) & jnp.logical_not(other) & beside))
        go = tuple(todo & g for g in wanted(q, other, p))

        @pl.when(p == 0)
        def _():
            copies = model_routes(slot)

            @pl.when(todo)
            def _():
                copies[2].wait_recv()

            begin(copies, go)
            cols = pl.ds(pl.multiple_of(slot * feats, 128), feats)
            weights = pmb[slot]
            macc[0] += jnp.dot(io_v[0, :, cols], weights, preferred_element_type=F32)
            macc[1] += jnp.dot(io_v[1, :, cols], weights, preferred_element_type=F32)

        @pl.when(p > 0)
        def _():
            copies = hidden_routes(slot, p)

            @pl.when(todo)
            def _():
                copies[2].wait_recv()

            begin(copies, go)

            @pl.when(end & jnp.logical_not(other) & (q == 1) & (p == UP))
            def _():
                part = rows_of(slot, UP, 0, SPLIT)
                remote(part, part, slot, UP, w_sem.at[2], across).start()

            @pl.when(jnp.logical_not(end) & jnp.logical_not(other) & (q == nz - 1) & (p == GATE))
            def _():
                for late, of, start in ((UP, across, SPLIT), (GATE, me, 0), (GATE, across, 0)):
                    part = rows_of(of, late, start, 64 - start)
                    remote(part, part, of, late, w_sem.at[1], outward).start()

            wacc[p - 1] += lax.dot_general(
                rows_of(slot, p)[...], act[p - 1, slot], NT, preferred_element_type=F32
            )

        @pl.when(i == jnp.where(end, MODEL_SENT[0], MODEL_SENT[1]))
        def _():
            send_model()

        @pl.when(i == jnp.where(end, MODEL_SUMMED[0], MODEL_SUMMED[1]))
        def _():
            sum_model()

        @pl.when(i == jnp.where(end, HID_DONE[0], HID_DONE[1]))
        def _():
            features_out()

        at_up = i == jnp.where(end, UP_DONE[0], UP_DONE[1])

        @pl.when(at_up | (i == len(END) - 1))
        def _():
            features_in(jnp.where(at_up, 1, 2))

        return carry

    lax.fori_loop(0, len(END), event, 0)

    def all_sent(ref, sem):
        pltpu.make_async_remote_copy(
            src_ref=ref, dst_ref=ref, send_sem=sem, recv_sem=recv.at[me, PM],
            device_id=(across, t), device_id_type=MESH,
        ).wait_send()

    def sent(k, blocks, rows):
        all_sent(pmb.at[pl.ds(0, blocks)], p_sem.at[k])
        all_sent(wtb.at[pl.ds(0, rows), :], w_sem.at[k])

    @pl.when(end)
    def _():
        sent(0, 1, 384)
        sent(2, 4, 640 + SPLIT)

    @pl.when(jnp.logical_not(end))
    def _():
        sent(0, 2, 384)
        sent(1, 3, 704 - SPLIT)
        sent(2, 4, 576)

    mate_copy.wait_send()
    far_both.wait_send()
    for k in range(3):
        total = ftx[k, t]
        feature_wait(frx.at[k], k).wait_recv()
        for j in range(1, nt):
            total = total + frx[k, j - 1]
        out[pl.ds(32 * (2, 1, 0)[k], 32), :] = total
    feature_wait(frx, 0).wait_send()


def fused(
    nz, nx, ny,
    inputs, out_grads, gate_pre, up_pre, hidden_grad, proj_model, proj_hidden, lengths, owners,
):
    ndp = nz * nx
    nt = 2 * ny
    toks, wide = inputs.shape
    units, feats = proj_hidden.shape[0], proj_model.shape[0]
    hbm = pl.BlockSpec(memory_space=pltpu.HBM)
    dma = pltpu.SemaphoreType.DMA
    out = pl.pallas_call(
        functools.partial(kernel, nz, nx, ny),
        out_shape=pltpu.VMEM((96, 128), F32),
        in_specs=[hbm] * 9,
        out_specs=pl.BlockSpec(memory_space=pltpu.VMEM),
        scratch_shapes=[
            pltpu.VMEM((ndp, 3, toks, units), BF16),
            pltpu.VMEM((3, ndp, toks, units), BF16),
            pltpu.VMEM((2, toks, wide), BF16),
            pltpu.VMEM((ndp, feats, 128), BF16),
            pltpu.VMEM((ndp * 192, units), BF16),
            pltpu.VMEM((2, toks, 128), F32),
            pltpu.VMEM((3, 64, toks), F32),
            pltpu.VMEM((toks, 128), F32),
            pltpu.VMEM((toks, 128), BF16),
            pltpu.VMEM((toks, 128), F32),
            pltpu.VMEM((2, toks, 128), BF16),
            pltpu.VMEM((2, 2, toks, 64 * nt), BF16),
            pltpu.VMEM((nt // 2, 64, 128), F32),
            pltpu.VMEM((64 * nt, 128), F32),
            pltpu.VMEM((3, nt, 32, 128), F32),
            pltpu.VMEM((3, nt - 1, 32, 128), F32),
            pltpu.SMEM((1, nt), jnp.int32),
            pltpu.SMEM((1, nt), jnp.int32),
            dma((ndp,)),
            dma((1,)),
            dma((4,)),
            dma((ndp, 4)),
            dma((3,)),
            dma((3,)),
            dma((2,)),
            dma((2,)),
            dma((1,)),
            dma((3,)),
        ],
        compiler_params=pltpu.CompilerParams(
            collective_id=0, has_side_effects=True, vmem_limit_bytes=60416 << 10
        ),
    )(inputs, out_grads, gate_pre, up_pre, hidden_grad, proj_model, proj_hidden.T, lengths, owners)
    return out.reshape(1, 3 * 64 * 64)


def per_device(
    inputs, out_grads, gate_pre, up_pre, hidden_grad, proj_model, proj_hidden, lengths, owners
):
    rank_width = proj_model.shape[1] // 2
    tok_rows = inputs.shape[0]
    gate_value = gate_pre.astype(jnp.float32)
    up_value = up_pre.astype(jnp.float32)
    grad_value = hidden_grad.astype(jnp.float32)
    sigmoid_gate = jax.nn.sigmoid(gate_value)
    hidden = (gate_value * sigmoid_gate * up_value).astype(jnp.bfloat16)
    up_grad = (grad_value * gate_value * sigmoid_gate).astype(jnp.bfloat16)
    gate_grad = (
        grad_value * up_value * sigmoid_gate * (1.0 + gate_value * (1.0 - sigmoid_gate))
    ).astype(jnp.bfloat16)
    sources = (gate_grad, up_grad, hidden)
    block_rows = lax.all_gather(proj_hidden, "dp", axis=0, tiled=True)
    parts = []
    for column, source in enumerate(sources):
        parts.append(
            jnp.dot(
                source,
                block_rows[:, column * rank_width : (column + 1) * rank_width],
                preferred_element_type=jnp.float32,
            )
        )
    hidden_part = jnp.concatenate(parts, axis=1)
    block_rows = lax.all_gather(proj_model, "dp", axis=0, tiled=True)
    first_part = jnp.dot(inputs, block_rows[:, :rank_width], preferred_element_type=jnp.float32)
    second_part = jnp.dot(out_grads, block_rows[:, rank_width:], preferred_element_type=jnp.float32)
    model_part = jnp.concatenate([first_part, second_part], axis=1)
    partial_value = jnp.concatenate([hidden_part, model_part], axis=1)
    lens = lengths[0]
    owner_row = owners[0]
    order = jnp.arange(lens.shape[0], dtype=jnp.int32)
    starts = jnp.sum(jnp.where(order[None, :] < order[:, None], lens[None, :], 0), axis=1)
    myself = lax.axis_index("tensor")
    tensor_count = lax.axis_size("tensor")
    chosen = (owner_row == myself).astype(jnp.int32)
    my_length = jnp.sum(lens * chosen)
    capacity = 3 * tok_rows // tensor_count
    slots = jnp.arange(capacity * lax.axis_size("tensor"), dtype=jnp.int32)
    holder = slots // capacity
    within = slots % capacity
    matched = (owner_row[None, :] == holder[:, None]).astype(jnp.int32)
    first_token = jnp.sum(matched * starts[None, :], axis=1)
    span = jnp.sum(matched * lens[None, :], axis=1)
    valid = within < span
    picked = jnp.where(valid, first_token + within, 0)
    summed = lax.psum_scatter(
        jnp.take(partial_value, picked, axis=0) * valid[:, None].astype(jnp.float32),
        "tensor",
        scatter_dimension=0,
        tiled=True,
    )
    weights = (jnp.arange(capacity, dtype=jnp.int32) < my_length).astype(jnp.float32)

    def block_of(index):
        return summed[:, index * rank_width : (index + 1) * rank_width]

    pairs = ((0, 3), (1, 3), (4, 2))
    blocks = []
    for left_index, right_index in pairs:
        left_side = block_of(left_index) * weights[:, None]
        blocks.append(
            jnp.einsum(
                "ta,tb->ab", left_side, block_of(right_index), precision=lax.Precision.HIGHEST
            )
        )
    return jnp.stack(blocks, axis=0).reshape(1, 3 * rank_width * rank_width)


def solution(mesh):
    in_specs = (
        P("dp", "tensor"),
        P("dp", "tensor"),
        P("dp", "tensor"),
        P("dp", "tensor"),
        P("dp", "tensor"),
        P(("tensor", "dp"), None),
        P(("tensor", "dp"), None),
        P("dp", None),
        P("dp", None),
    )
    out_specs = P(("dp", "tensor"), None)
    ndp, ny = mesh.shape["dp"], mesh.shape["tensor"] // 2

    def program(*args):
        units, feats, rank_width = args[6].shape[0], args[5].shape[0], args[5].shape[1] // 2
        nx = math.isqrt(ndp // 2)
        fits = units % 128 == 0 and feats % 128 == 0 and rank_width == 64 and args[0].shape[0] % 128 == 0
        if fits and (nx, ny) == (2, 2) and ndp == 4 * nx:
            return fused(ndp // nx, nx, ny, *args)
        return per_device(*args)

    return jax.shard_map(
        program, mesh=mesh, in_specs=in_specs, out_specs=out_specs, check_vma=False
    )
```

```python
import functools
import math

import jax
import jax.numpy as jnp
from jax import lax
from jax.experimental import pallas as pl
from jax.experimental.pallas import tpu as pltpu
from jax.sharding import PartitionSpec as P

MESH = pl.DeviceIdType.MESH
NT = (((1,), (1,)), ((), ()))
F32 = jnp.float32
BF16 = jnp.bfloat16
ROWS = 32
PM, HID, UP, GATE = range(4)
END = (
    (0, 0, PM), (0, 0, HID), (0, 1, HID), (0, 1, UP),
    (2, 0, PM), (0, 0, UP), (0, 0, GATE), (1, 0, PM),
    (1, 0, HID), (0, 1, PM), (1, 1, PM), (2, 0, HID),
    (0, 1, GATE), (2, 0, UP), (1, 1, HID), (3, 0, PM),
    (2, 1, PM), (2, 0, GATE), (2, 1, HID), (3, 0, HID),
    (2, 1, UP), (3, 0, UP), (3, 1, PM), (3, 0, GATE),
    (2, 1, GATE), (1, 0, UP), (3, 1, HID), (1, 1, UP),
    (3, 1, UP), (1, 0, GATE), (1, 1, GATE), (3, 1, GATE),
)
MID = (
    (2, 0, UP), (0, 0, UP), (1, 0, PM), (1, 0, HID),
    (3, 0, PM), (1, 0, UP), (1, 0, GATE), (0, 0, PM),
    (2, 0, PM), (0, 0, GATE), (2, 0, HID), (2, 0, GATE),
    (0, 0, HID), (1, 1, PM), (1, 1, HID), (1, 1, UP),
    (0, 1, PM), (2, 1, PM), (3, 0, HID), (1, 1, GATE),
    (0, 1, HID), (3, 0, UP), (2, 1, HID), (3, 1, PM),
    (3, 0, GATE), (2, 1, UP), (2, 1, GATE), (0, 1, UP),
    (3, 1, HID), (0, 1, GATE), (3, 1, UP), (3, 1, GATE),
)
MODEL_SENT = (22, 25)
MODEL_SUMMED = (26, 29)
HID_DONE = (26, 29)
UP_DONE = (28, 30)
SHIPPED, HELPED = 2, 26
PER = 6


def packed(events):
    words = []
    for at in range(0, len(events), PER):
        word = 0
        for j, (plane, other, piece) in enumerate(events[at : at + PER]):
            word += ((plane + 4 * other) * 4 + piece) << (5 * j)
        words.append(word)
    return words


def kernel(
    nz, nx, ny,
    inp_h, og_h, gp_h, up_h, hg_h, pm_h, wt_h, lens_h, owns_h,
    out,
    raw, act, io_v, pmb, wtb, macc, wacc, mtx, mtxb, mrx, mrxb, mm, fs, fh, ftx, frx, guest, gtx, grx, lens, owns,
    raw_sem, io_sem, own_sem, recv, w_sem, p_sem, g_sem, mt_sem, mr_sem, ft_sem, fr_sem,
):
    ndp = nz * nx
    nt = 2 * ny
    me = lax.axis_index("dp")
    t = lax.axis_index("tensor")
    z, x = me // nx, me % nx
    low_half = z < nz // 2
    r = jnp.where(low_half, z, nz - 1 - z)
    inward = me + jnp.where(low_half, nx, -nx)
    outward = me - jnp.where(low_half, nx, -nx)
    across = z * nx + 1 - x
    end = r == 0
    units = wt_h.shape[1]
    feats = pm_h.shape[0]
    toks = inp_h.shape[0]
    sources = (gp_h, up_h, hg_h)

    def raw_copy(block, q):
        cols = pl.ds(block * units, units)
        return pltpu.make_async_copy(sources[q].at[:, cols], raw.at[block, q], raw_sem.at[block])

    io = (pltpu.make_async_copy(inp_h, io_v.at[0], io_sem.at[0]),
          pltpu.make_async_copy(og_h, io_v.at[1], io_sem.at[0]))

    barrier = pltpu.get_barrier_semaphore()

    def greet(d, s):
        pl.semaphore_signal(barrier, inc=1, device_id=(d, s), device_id_type=MESH)

    greet(across, t)
    greet(inward, t)

    @pl.when(jnp.logical_not(end))
    def _():
        greet(outward, t)

    for j in range(1, nt):
        greet(me, (t + j) % nt)
    for block in range(ndp):
        for q in range(3):
            raw_copy(block, q).start()
    pl.semaphore_wait(barrier, nt + 1 + r)

    def rows_of(slot, p, first=0, count=64):
        return wtb.at[pl.ds(pl.multiple_of(slot * 192 + (3 - p) * 64 + first, 16), count), :]

    def remote(src, dst, slot, p, sem, d):
        return pltpu.make_async_remote_copy(
            src_ref=src, dst_ref=dst, send_sem=sem, recv_sem=recv.at[slot, p],
            device_id=(d, t), device_id_type=MESH,
        )

    def routes(src, dst, slot, p, sems):
        return tuple(
            remote(src, dst, slot, p, sems.at[k], d) for k, d in enumerate((inward, outward, across))
        )

    def model_routes(slot):
        return routes(pmb.at[slot], pmb.at[slot], slot, PM, p_sem)

    def hidden_routes(slot, p):
        return routes(rows_of(slot, p), rows_of(slot, p), slot, p, w_sem)

    def wanted(q, other, p):
        same = jnp.logical_not(other)
        mid = jnp.logical_not(end)
        go_in = (mid & same & (q == 0)) | (end & other & (q == 0) & (p > 0))
        go_out = mid & same & (q >= 2)
        go_x = same & ((end & ((q >= 2) | (p <= HID))) | (mid & ((q >= 2) | (p == 0))))
        return go_in, go_out, go_x

    def slot_of(q, other):
        return jnp.where(low_half, q, nz - 1 - q) * nx + jnp.where(other, 1 - x, x)

    def begin(copies, conditions):
        for copy, condition in zip(copies, conditions):
            @pl.when(condition)
            def _():
                copy.start()

    def send_own(p):
        if p is PM:
            copies = routes(pm_h, pmb.at[me], me, PM, p_sem)
        else:
            own = wt_h.at[pl.ds((3 - p) * 64, 64), :]
            copies = routes(own, rows_of(me, p), me, p, w_sem)
        copies[0].start()
        if p is not GATE:
            @pl.when(jnp.logical_not(end))
            def _():
                copies[1].start()
        copies[2].start()

    for p in (PM, HID, UP):
        send_own(p)
    keep = (
        pltpu.make_async_copy(pm_h, pmb.at[me], own_sem.at[0]),
        pltpu.make_async_copy(lens_h, lens, own_sem.at[2]),
        pltpu.make_async_copy(owns_h, owns, own_sem.at[3]),
        pltpu.make_async_copy(wt_h, wtb.at[pl.ds(pl.multiple_of(me * 192, 64), 192), :], own_sem.at[1]),
    )
    for copy in keep:
        copy.start()
    for copy in io:
        copy.start()
    macc[...] = jnp.zeros_like(macc)
    wacc[...] = jnp.zeros_like(wacc)

    def near(q, p):
        slot = slot_of(q, False)
        copies = model_routes(slot) if p is PM else hidden_routes(slot, p)
        copies[2].wait_recv()
        begin(copies, wanted(jnp.int32(q), False, p))

    def elementwise(block, carry):
        for at, p in ((ndp // 2, PM), (3 * ndp // 4, HID)):
            @pl.when((block == at) & end)
            def _():
                near(1, p)

            @pl.when((block == at) & jnp.logical_not(end))
            def _():
                near(2, p)
                near(0, p)

        @pl.when(block == ndp // 2)
        def _():
            send_own(GATE)

        pltpu.make_async_copy(raw.at[block], raw.at[block], raw_sem.at[block]).wait()

        def some(i, carry):
            rows = pl.ds(pl.multiple_of(i * ROWS, ROWS), ROWS)
            gate = raw[block, 0, rows, :].astype(F32)
            up = raw[block, 1, rows, :].astype(F32)
            grad = raw[block, 2, rows, :].astype(F32)
            sig = 0.5 * jnp.tanh(0.5 * gate) + 0.5
            silu = gate * sig
            act[0, block, rows, :] = (silu * up).astype(BF16)
            act[1, block, rows, :] = (grad * silu).astype(BF16)
            act[2, block, rows, :] = (grad * up * (sig + silu * (1.0 - sig))).astype(BF16)
            return carry

        lax.fori_loop(0, toks // ROWS, some, 0)
        return carry

    lax.fori_loop(0, ndp, elementwise, 0)
    pltpu.make_async_copy(io_v, io_v, io_sem.at[0]).wait()
    for copy in keep:
        copy.wait()

    first_lanes = lax.broadcasted_iota(jnp.int32, (toks, 128), 1) < 64
    first = lax.broadcasted_iota(jnp.int32, (32, 128), 1) < 64

    c = t % 2
    y = t // 2
    mate_copy = pltpu.make_async_remote_copy(
        src_ref=mtx, dst_ref=mrx, send_sem=mt_sem.at[0], recv_sem=mr_sem.at[0],
        device_id=(me, y * 2 + 1 - c), device_id_type=MESH,
    )
    far_copies = [
        pltpu.make_async_remote_copy(
            src_ref=mtxb, dst_ref=mrxb.at[j], send_sem=mt_sem.at[1], recv_sem=mr_sem.at[1],
            device_id=(me, (1 - y) * 2 + (c + j) % 2), device_id_type=MESH,
        )
        for j in range(2)
    ]
    far_both = pltpu.make_async_remote_copy(
        src_ref=mrxb, dst_ref=mrxb, send_sem=mt_sem.at[1], recv_sem=mr_sem.at[1],
        device_id=(me, (1 - y) * 2 + c), device_id_type=MESH,
    )

    def send_model():
        both = jnp.where(first_lanes, macc[0], macc[1])
        mtx[...] = both
        mtxb[...] = both.astype(BF16)
        for copy in far_copies:
            copy.start()
        mate_copy.start()

    def sum_model():
        mate_copy.wait_recv()
        far_both.wait_recv()
        full = mtx[...] + mrx[...] + (mrxb[0].astype(F32) + mrxb[1].astype(F32))
        turned = pltpu.roll(full, 64, 1)
        pair = (jnp.where(first_lanes, full, turned), jnp.where(first_lanes, turned, full))
        starts, stops = [], []
        for s in range(nt):
            start, stop, seen = jnp.int32(0), jnp.int32(0), jnp.int32(0)
            for e in range(nt):
                hit = owns[0, e] == s
                start = jnp.where(hit, seen, start)
                seen = seen + lens[0, e]
                stop = jnp.where(hit, seen, stop)
            starts.append(start)
            stops.append(stop)
        token = lax.broadcasted_iota(jnp.int32, (toks, 128), 0)
        for h in range(nt // 2):
            start = jnp.where(first_lanes, starts[2 * h], starts[2 * h + 1])
            stop = jnp.where(first_lanes, stops[2 * h], stops[2 * h + 1])
            inside = (token >= start) & (token < stop)
            for side in range(2):
                value = jnp.where(inside, pair[side], 0.0)
                high = value.astype(BF16)
                mm[side, 0, :, pl.ds(128 * h, 128)] = high
                mm[side, 1, :, pl.ds(128 * h, 128)] = (value - high.astype(F32)).astype(BF16)

    def products(k, side):
        value = wacc[k]
        high = value.astype(BF16)
        rest = (value - high.astype(F32)).astype(BF16)

        def dot(left, right):
            return jnp.dot(left, right, preferred_element_type=F32)

        return dot(high, mm[side, 0]) + (dot(high, mm[side, 1]) + dot(rest, mm[side, 0]))

    def feature_copy(k, j):
        s = (t + j) % nt
        return pltpu.make_async_remote_copy(
            src_ref=ftx.at[k, s], dst_ref=frx.at[k, j - 1], send_sem=ft_sem.at[0],
            recv_sem=fr_sem.at[k], device_id=(me, s), device_id_type=MESH,
        )

    def feature_wait(ref, k):
        return pltpu.make_async_remote_copy(
            src_ref=ref, dst_ref=ref, send_sem=ft_sem.at[0], recv_sem=fr_sem.at[k],
            device_id=(me, (t + 1) % nt), device_id_type=MESH,
        )

    def send_features(k):
        for j in range(1, nt):
            feature_copy(k, j).start()

    def features_in(k):
        value = products(k, 0)
        for h in range(nt // 2):
            fs[h] = value[:, 128 * h : 128 * h + 128]
            even = fs[h, pl.ds(0, 32, stride=2), :]
            odd = fs[h, pl.ds(1, 32, stride=2), :]
            ftx[k, 2 * h] = jnp.where(first, even, pltpu.roll(odd, 64, 1))
            ftx[k, 2 * h + 1] = jnp.where(first, pltpu.roll(even, 64, 1), odd)
        send_features(k)

    def features_out():
        fh[:, pl.ds(0, 64)] = products(0, 1).T
        for s in range(nt):
            even = fh[pl.ds(64 * s, 32, stride=2), :]
            odd = fh[pl.ds(64 * s + 1, 32, stride=2), :]
            ftx[0, s] = jnp.concatenate([even[:, :64], odd[:, :64]], axis=1)
        send_features(0)

    words = [jnp.where(end, jnp.int32(a), jnp.int32(b)) for a, b in zip(packed(END), packed(MID))]

    def decode(i):
        word = words[0]
        for j in range(1, len(words)):
            word = jnp.where(i // PER == j, words[j], word)
        code = lax.shift_right_logical(word, 5 * (i % PER)) % 32
        return (code // 4) % 4, code // 16 == 1, code % 4

    beside_slot = slot_of(1, False)

    def ship():
        return remote(act.at[GATE - 1, beside_slot], guest, beside_slot, PM, g_sem.at[0], inward)

    def help_back(slot):
        return remote(gtx, grx, slot, GATE, g_sem.at[1], outward)

    def send_late(p):
        part = rows_of(across, p)
        remote(part, part, across, p, w_sem.at[1], outward).start()

    def event(i, carry):
        q, other, p = decode(i)
        slot = slot_of(q, other)
        mine = jnp.logical_not(other) & (q == r)
        beside = (q - r == 1) | (r - q == 1)
        todo = jnp.logical_not(mine | ((p <= HID) & jnp.logical_not(other) & beside))
        go = tuple(todo & g for g in wanted(q, other, p))

        @pl.when(p == 0)
        def _():
            copies = model_routes(slot)

            @pl.when(todo)
            def _():
                copies[2].wait_recv()

            begin(copies, go)
            cols = pl.ds(pl.multiple_of(slot * feats, 128), feats)
            weights = pmb[slot]
            macc[0] += jnp.dot(io_v[0, :, cols], weights, preferred_element_type=F32)
            macc[1] += jnp.dot(io_v[1, :, cols], weights, preferred_element_type=F32)

        @pl.when(p > 0)
        def _():
            copies = hidden_routes(slot, p)

            helped = end & jnp.logical_not(other) & (q == 1) & (p == GATE)

            @pl.when(todo & jnp.logical_not(helped))
            def _():
                copies[2].wait_recv()

            begin(copies, go)

            @pl.when(jnp.logical_not(end) & jnp.logical_not(other) & (q == nz - 1) & (p == GATE))
            def _():
                send_late(UP)

            @pl.when(helped)
            def _():
                help_back(beside_slot).wait_recv()
                wacc[GATE - 1] += grx[...].astype(F32)

            @pl.when(jnp.logical_not(helped))
            def _():
                wacc[p - 1] += lax.dot_general(
                    rows_of(slot, p)[...], act[p - 1, slot], NT, preferred_element_type=F32
                )

        @pl.when(end & (i == SHIPPED))
        def _():
            ship().start()

        @pl.when(jnp.logical_not(end) & (i == HELPED))
        def _():
            ship().wait_recv()
            gtx[...] = lax.dot_general(
                rows_of(me, GATE)[...], guest[...], NT, preferred_element_type=F32
            ).astype(BF16)
            help_back(me).start()
            send_late(GATE)

        @pl.when(i == jnp.where(end, MODEL_SENT[0], MODEL_SENT[1]))
        def _():
            send_model()

        @pl.when(i == jnp.where(end, MODEL_SUMMED[0], MODEL_SUMMED[1]))
        def _():
            sum_model()

        @pl.when(i == jnp.where(end, HID_DONE[0], HID_DONE[1]))
        def _():
            features_out()

        at_up = i == jnp.where(end, UP_DONE[0], UP_DONE[1])

        @pl.when(at_up | (i == len(END) - 1))
        def _():
            features_in(jnp.where(at_up, 1, 2))

        return carry

    lax.fori_loop(0, len(END), event, 0)

    def all_sent(ref, sem):
        pltpu.make_async_remote_copy(
            src_ref=ref, dst_ref=ref, send_sem=sem, recv_sem=recv.at[me, PM],
            device_id=(across, t), device_id_type=MESH,
        ).wait_send()

    def sent(k, blocks, rows):
        all_sent(pmb.at[pl.ds(0, blocks)], p_sem.at[k])
        all_sent(wtb.at[pl.ds(0, rows), :], w_sem.at[k])

    @pl.when(end)
    def _():
        sent(0, 1, 384)
        sent(2, 4, 640)
        ship().wait_send()

    @pl.when(jnp.logical_not(end))
    def _():
        sent(0, 2, 384)
        sent(1, 3, 640)
        help_back(me).wait_send()
        sent(2, 4, 576)

    mate_copy.wait_send()
    far_both.wait_send()
    for k in range(3):
        total = ftx[k, t]
        feature_wait(frx.at[k], k).wait_recv()
        for j in range(1, nt):
            total = total + frx[k, j - 1]
        out[pl.ds(32 * (2, 1, 0)[k], 32), :] = total
    feature_wait(frx, 0).wait_send()


def fused(
    nz, nx, ny,
    inputs, out_grads, gate_pre, up_pre, hidden_grad, proj_model, proj_hidden, lengths, owners,
):
    ndp = nz * nx
    nt = 2 * ny
    toks, wide = inputs.shape
    units, feats = proj_hidden.shape[0], proj_model.shape[0]
    hbm = pl.BlockSpec(memory_space=pltpu.HBM)
    dma = pltpu.SemaphoreType.DMA
    out = pl.pallas_call(
        functools.partial(kernel, nz, nx, ny),
        out_shape=pltpu.VMEM((96, 128), F32),
        in_specs=[hbm] * 9,
        out_specs=pl.BlockSpec(memory_space=pltpu.VMEM),
        scratch_shapes=[
            pltpu.VMEM((ndp, 3, toks, units), BF16),
            pltpu.VMEM((3, ndp, toks, units), BF16),
            pltpu.VMEM((2, toks, wide), BF16),
            pltpu.VMEM((ndp, feats, 128), BF16),
            pltpu.VMEM((ndp * 192, units), BF16),
            pltpu.VMEM((2, toks, 128), F32),
            pltpu.VMEM((3, 64, toks), F32),
            pltpu.VMEM((toks, 128), F32),
            pltpu.VMEM((toks, 128), BF16),
            pltpu.VMEM((toks, 128), F32),
            pltpu.VMEM((2, toks, 128), BF16),
            pltpu.VMEM((2, 2, toks, 64 * nt), BF16),
            pltpu.VMEM((nt // 2, 64, 128), F32),
            pltpu.VMEM((64 * nt, 128), F32),
            pltpu.VMEM((3, nt, 32, 128), F32),
            pltpu.VMEM((3, nt - 1, 32, 128), F32),
            pltpu.VMEM((toks, units), BF16),
            pltpu.VMEM((64, toks), BF16),
            pltpu.VMEM((64, toks), BF16),
            pltpu.SMEM((1, nt), jnp.int32),
            pltpu.SMEM((1, nt), jnp.int32),
            dma((ndp,)),
            dma((1,)),
            dma((4,)),
            dma((ndp, 4)),
            dma((3,)),
            dma((3,)),
            dma((2,)),
            dma((2,)),
            dma((2,)),
            dma((1,)),
            dma((3,)),
        ],
        compiler_params=pltpu.CompilerParams(
            collective_id=0, has_side_effects=True, vmem_limit_bytes=60416 << 10
        ),
    )(inputs, out_grads, gate_pre, up_pre, hidden_grad, proj_model, proj_hidden.T, lengths, owners)
    return out.reshape(1, 3 * 64 * 64)


def per_device(
    inputs, out_grads, gate_pre, up_pre, hidden_grad, proj_model, proj_hidden, lengths, owners
):
    rank_width = proj_model.shape[1] // 2
    tok_rows = inputs.shape[0]
    gate_value = gate_pre.astype(jnp.float32)
    up_value = up_pre.astype(jnp.float32)
    grad_value = hidden_grad.astype(jnp.float32)
    sigmoid_gate = jax.nn.sigmoid(gate_value)
    hidden = (gate_value * sigmoid_gate * up_value).astype(jnp.bfloat16)
    up_grad = (grad_value * gate_value * sigmoid_gate).astype(jnp.bfloat16)
    gate_grad = (
        grad_value * up_value * sigmoid_gate * (1.0 + gate_value * (1.0 - sigmoid_gate))
    ).astype(jnp.bfloat16)
    sources = (gate_grad, up_grad, hidden)
    block_rows = lax.all_gather(proj_hidden, "dp", axis=0, tiled=True)
    parts = []
    for column, source in enumerate(sources):
        parts.append(
            jnp.dot(
                source,
                block_rows[:, column * rank_width : (column + 1) * rank_width],
                preferred_element_type=jnp.float32,
            )
        )
    hidden_part = jnp.concatenate(parts, axis=1)
    block_rows = lax.all_gather(proj_model, "dp", axis=0, tiled=True)
    first_part = jnp.dot(inputs, block_rows[:, :rank_width], preferred_element_type=jnp.float32)
    second_part = jnp.dot(out_grads, block_rows[:, rank_width:], preferred_element_type=jnp.float32)
    model_part = jnp.concatenate([first_part, second_part], axis=1)
    partial_value = jnp.concatenate([hidden_part, model_part], axis=1)
    lens = lengths[0]
    owner_row = owners[0]
    order = jnp.arange(lens.shape[0], dtype=jnp.int32)
    starts = jnp.sum(jnp.where(order[None, :] < order[:, None], lens[None, :], 0), axis=1)
    myself = lax.axis_index("tensor")
    tensor_count = lax.axis_size("tensor")
    chosen = (owner_row == myself).astype(jnp.int32)
    my_length = jnp.sum(lens * chosen)
    capacity = 3 * tok_rows // tensor_count
    slots = jnp.arange(capacity * lax.axis_size("tensor"), dtype=jnp.int32)
    holder = slots // capacity
    within = slots % capacity
    matched = (owner_row[None, :] == holder[:, None]).astype(jnp.int32)
    first_token = jnp.sum(matched * starts[None, :], axis=1)
    span = jnp.sum(matched * lens[None, :], axis=1)
    valid = within < span
    picked = jnp.where(valid, first_token + within, 0)
    summed = lax.psum_scatter(
        jnp.take(partial_value, picked, axis=0) * valid[:, None].astype(jnp.float32),
        "tensor",
        scatter_dimension=0,
        tiled=True,
    )
    weights = (jnp.arange(capacity, dtype=jnp.int32) < my_length).astype(jnp.float32)

    def block_of(index):
        return summed[:, index * rank_width : (index + 1) * rank_width]

    pairs = ((0, 3), (1, 3), (4, 2))
    blocks = []
    for left_index, right_index in pairs:
        left_side = block_of(left_index) * weights[:, None]
        blocks.append(
            jnp.einsum(
                "ta,tb->ab", left_side, block_of(right_index), precision=lax.Precision.HIGHEST
            )
        )
    return jnp.stack(blocks, axis=0).reshape(1, 3 * rank_width * rank_width)


def solution(mesh):
    in_specs = (
        P("dp", "tensor"),
        P("dp", "tensor"),
        P("dp", "tensor"),
        P("dp", "tensor"),
        P("dp", "tensor"),
        P(("tensor", "dp"), None),
        P(("tensor", "dp"), None),
        P("dp", None),
        P("dp", None),
    )
    out_specs = P(("dp", "tensor"), None)
    ndp, ny = mesh.shape["dp"], mesh.shape["tensor"] // 2

    def program(*args):
        units, feats, rank_width = args[6].shape[0], args[5].shape[0], args[5].shape[1] // 2
        nx = math.isqrt(ndp // 2)
        fits = units % 128 == 0 and feats % 128 == 0 and rank_width == 64 and args[0].shape[0] % 128 == 0
        if fits and (nx, ny) == (2, 2) and ndp == 4 * nx:
            return fused(ndp // nx, nx, ny, *args)
        return per_device(*args)

    return jax.shard_map(
        program, mesh=mesh, in_specs=in_specs, out_specs=out_specs, check_vma=False
    )
```

```python
import functools
import math

import jax
import jax.numpy as jnp
from jax import lax
from jax.experimental import pallas as pl
from jax.experimental.pallas import tpu as pltpu
from jax.sharding import PartitionSpec as P

MESH = pl.DeviceIdType.MESH
NT = (((1,), (1,)), ((), ()))
F32 = jnp.float32
BF16 = jnp.bfloat16
ROWS = 32
PM, HID, UP, GATE = range(4)
END = (
    (0, 0, PM), (0, 0, HID), (0, 1, HID), (2, 0, PM),
    (0, 1, UP), (0, 0, UP), (0, 0, GATE), (1, 0, PM),
    (1, 0, HID), (0, 1, PM), (1, 1, PM), (2, 0, HID),
    (0, 1, GATE), (2, 0, UP), (1, 1, HID), (3, 0, PM),
    (2, 1, PM), (2, 0, GATE), (2, 1, HID), (3, 0, HID),
    (2, 1, UP), (3, 0, UP), (3, 1, PM), (3, 0, GATE),
    (2, 1, GATE), (1, 0, UP), (3, 1, HID), (1, 1, UP),
    (3, 1, UP), (1, 0, GATE), (1, 1, GATE), (3, 1, GATE),
)
MID = (
    (2, 0, UP), (0, 0, UP), (1, 0, PM), (1, 0, HID),
    (3, 0, PM), (1, 0, UP), (1, 0, GATE), (0, 0, PM),
    (2, 0, PM), (0, 0, GATE), (2, 0, HID), (2, 0, GATE),
    (0, 0, HID), (1, 1, PM), (1, 1, HID), (1, 1, UP),
    (0, 1, PM), (2, 1, PM), (3, 0, HID), (1, 1, GATE),
    (0, 1, HID), (3, 0, UP), (2, 1, HID), (3, 1, PM),
    (3, 0, GATE), (2, 1, UP), (2, 1, GATE), (0, 1, UP),
    (3, 1, HID), (0, 1, GATE), (3, 1, UP), (3, 1, GATE),
)
MODEL_SENT = (22, 25)
MODEL_SUMMED = (26, 29)
HID_DONE = (26, 29)
UP_DONE = (28, 30)
SHIPPED, HELPED = 2, 26
PER = 6


def packed(events):
    words = []
    for at in range(0, len(events), PER):
        word = 0
        for j, (plane, other, piece) in enumerate(events[at : at + PER]):
            word += ((plane + 4 * other) * 4 + piece) << (5 * j)
        words.append(word)
    return words


def kernel(
    nz, nx, ny,
    inp_h, og_h, gp_h, up_h, hg_h, pm_h, wt_h, lens_h, owns_h,
    out,
    raw, act, io_v, pmb, wtb, macc, wacc, mtx, mtxb, mrx, mrxb, mm, fs, fh, ftx, frx, guest, gtx, grx, lens, owns,
    raw_sem, io_sem, own_sem, recv, w_sem, p_sem, g_sem, mt_sem, mr_sem, ft_sem, fr_sem,
):
    ndp = nz * nx
    nt = 2 * ny
    me = lax.axis_index("dp")
    t = lax.axis_index("tensor")
    z, x = me // nx, me % nx
    low_half = z < nz // 2
    r = jnp.where(low_half, z, nz - 1 - z)
    inward = me + jnp.where(low_half, nx, -nx)
    outward = me - jnp.where(low_half, nx, -nx)
    across = z * nx + 1 - x
    end = r == 0
    units = wt_h.shape[1]
    feats = pm_h.shape[0]
    toks = inp_h.shape[0]
    sources = (gp_h, up_h, hg_h)

    def raw_copy(block, q):
        cols = pl.ds(block * units, units)
        return pltpu.make_async_copy(sources[q].at[:, cols], raw.at[block, q], raw_sem.at[block])

    io = (pltpu.make_async_copy(inp_h, io_v.at[0], io_sem.at[0]),
          pltpu.make_async_copy(og_h, io_v.at[1], io_sem.at[0]))

    barrier = pltpu.get_barrier_semaphore()

    def greet(d, s):
        pl.semaphore_signal(barrier, inc=1, device_id=(d, s), device_id_type=MESH)

    greet(across, t)
    greet(inward, t)

    @pl.when(jnp.logical_not(end))
    def _():
        greet(outward, t)

    for j in range(1, nt):
        greet(me, (t + j) % nt)
    for block in range(ndp):
        for q in range(3):
            raw_copy(block, q).start()
    pl.semaphore_wait(barrier, nt + 1 + r)

    def rows_of(slot, p, first=0, count=64):
        return wtb.at[pl.ds(pl.multiple_of(slot * 192 + (3 - p) * 64 + first, 16), count), :]

    def remote(src, dst, slot, p, sem, d):
        return pltpu.make_async_remote_copy(
            src_ref=src, dst_ref=dst, send_sem=sem, recv_sem=recv.at[slot, p],
            device_id=(d, t), device_id_type=MESH,
        )

    def routes(src, dst, slot, p, sems):
        return tuple(
            remote(src, dst, slot, p, sems.at[k], d) for k, d in enumerate((inward, outward, across))
        )

    def model_routes(slot):
        return routes(pmb.at[slot], pmb.at[slot], slot, PM, p_sem)

    def hidden_routes(slot, p):
        return routes(rows_of(slot, p), rows_of(slot, p), slot, p, w_sem)

    def wanted(q, other, p):
        same = jnp.logical_not(other)
        mid = jnp.logical_not(end)
        go_in = (mid & same & (q == 0)) | (end & other & (q == 0) & (p > 0))
        go_out = mid & same & (q >= 2)
        go_x = same & ((end & ((q >= 2) | (p <= HID))) | (mid & ((q >= 2) | (p == 0))))
        return go_in, go_out, go_x

    def slot_of(q, other):
        return jnp.where(low_half, q, nz - 1 - q) * nx + jnp.where(other, 1 - x, x)

    def begin(copies, conditions):
        for copy, condition in zip(copies, conditions):
            @pl.when(condition)
            def _():
                copy.start()

    def send_own(p):
        if p is PM:
            copies = routes(pm_h, pmb.at[me], me, PM, p_sem)
        else:
            own = wt_h.at[pl.ds((3 - p) * 64, 64), :]
            copies = routes(own, rows_of(me, p), me, p, w_sem)
        if p is not GATE:
            @pl.when(jnp.logical_not(end))
            def _():
                copies[1].start()
        copies[2].start()
        copies[0].start()

    for p in (PM, HID, UP):
        send_own(p)
    keep = (
        pltpu.make_async_copy(pm_h, pmb.at[me], own_sem.at[0]),
        pltpu.make_async_copy(lens_h, lens, own_sem.at[2]),
        pltpu.make_async_copy(owns_h, owns, own_sem.at[3]),
        pltpu.make_async_copy(wt_h, wtb.at[pl.ds(pl.multiple_of(me * 192, 64), 192), :], own_sem.at[1]),
    )
    for copy in keep:
        copy.start()
    for copy in io:
        copy.start()
    macc[...] = jnp.zeros_like(macc)
    wacc[...] = jnp.zeros_like(wacc)

    def near(q, p):
        slot = slot_of(q, False)
        copies = model_routes(slot) if p is PM else hidden_routes(slot, p)
        copies[2].wait_recv()
        begin(copies, wanted(jnp.int32(q), False, p))

    def elementwise(block, carry):
        for at, p in ((ndp // 2, PM), (3 * ndp // 4, HID)):
            @pl.when((block == at) & end)
            def _():
                near(1, p)

            @pl.when((block == at) & jnp.logical_not(end))
            def _():
                near(2, p)
                near(0, p)

        @pl.when(block == ndp // 2)
        def _():
            send_own(GATE)

        pltpu.make_async_copy(raw.at[block], raw.at[block], raw_sem.at[block]).wait()

        def some(i, carry):
            rows = pl.ds(pl.multiple_of(i * ROWS, ROWS), ROWS)
            gate = raw[block, 0, rows, :].astype(F32)
            up = raw[block, 1, rows, :].astype(F32)
            grad = raw[block, 2, rows, :].astype(F32)
            sig = 0.5 * jnp.tanh(0.5 * gate) + 0.5
            silu = gate * sig
            act[0, block, rows, :] = (silu * up).astype(BF16)
            act[1, block, rows, :] = (grad * silu).astype(BF16)
            act[2, block, rows, :] = (grad * up * (sig + silu * (1.0 - sig))).astype(BF16)
            return carry

        lax.fori_loop(0, toks // ROWS, some, 0)
        return carry

    lax.fori_loop(0, ndp, elementwise, 0)
    pltpu.make_async_copy(io_v, io_v, io_sem.at[0]).wait()
    for copy in keep:
        copy.wait()

    first_lanes = lax.broadcasted_iota(jnp.int32, (toks, 128), 1) < 64
    first = lax.broadcasted_iota(jnp.int32, (32, 128), 1) < 64

    c = t % 2
    y = t // 2
    mate_copy = pltpu.make_async_remote_copy(
        src_ref=mtx, dst_ref=mrx, send_sem=mt_sem.at[0], recv_sem=mr_sem.at[0],
        device_id=(me, y * 2 + 1 - c), device_id_type=MESH,
    )
    far_copies = [
        pltpu.make_async_remote_copy(
            src_ref=mtxb, dst_ref=mrxb.at[j], send_sem=mt_sem.at[1], recv_sem=mr_sem.at[1],
            device_id=(me, (1 - y) * 2 + (c + j) % 2), device_id_type=MESH,
        )
        for j in range(2)
    ]
    far_both = pltpu.make_async_remote_copy(
        src_ref=mrxb, dst_ref=mrxb, send_sem=mt_sem.at[1], recv_sem=mr_sem.at[1],
        device_id=(me, (1 - y) * 2 + c), device_id_type=MESH,
    )

    def send_model():
        both = jnp.where(first_lanes, macc[0], macc[1])
        mtx[...] = both
        mtxb[...] = both.astype(BF16)
        for copy in far_copies:
            copy.start()
        mate_copy.start()

    def sum_model():
        mate_copy.wait_recv()
        far_both.wait_recv()
        full = mtx[...] + mrx[...] + (mrxb[0].astype(F32) + mrxb[1].astype(F32))
        turned = pltpu.roll(full, 64, 1)
        pair = (jnp.where(first_lanes, full, turned), jnp.where(first_lanes, turned, full))
        starts, stops = [], []
        for s in range(nt):
            start, stop, seen = jnp.int32(0), jnp.int32(0), jnp.int32(0)
            for e in range(nt):
                hit = owns[0, e] == s
                start = jnp.where(hit, seen, start)
                seen = seen + lens[0, e]
                stop = jnp.where(hit, seen, stop)
            starts.append(start)
            stops.append(stop)
        token = lax.broadcasted_iota(jnp.int32, (toks, 128), 0)
        for h in range(nt // 2):
            start = jnp.where(first_lanes, starts[2 * h], starts[2 * h + 1])
            stop = jnp.where(first_lanes, stops[2 * h], stops[2 * h + 1])
            inside = (token >= start) & (token < stop)
            for side in range(2):
                value = jnp.where(inside, pair[side], 0.0)
                high = value.astype(BF16)
                mm[side, 0, :, pl.ds(128 * h, 128)] = high
                mm[side, 1, :, pl.ds(128 * h, 128)] = (value - high.astype(F32)).astype(BF16)

    def products(k, side):
        value = wacc[k]
        high = value.astype(BF16)
        rest = (value - high.astype(F32)).astype(BF16)

        def dot(left, right):
            return jnp.dot(left, right, preferred_element_type=F32)

        return dot(high, mm[side, 0]) + (dot(high, mm[side, 1]) + dot(rest, mm[side, 0]))

    def feature_copy(k, j):
        s = (t + j) % nt
        return pltpu.make_async_remote_copy(
            src_ref=ftx.at[k, s], dst_ref=frx.at[k, j - 1], send_sem=ft_sem.at[0],
            recv_sem=fr_sem.at[k], device_id=(me, s), device_id_type=MESH,
        )

    def feature_wait(ref, k):
        return pltpu.make_async_remote_copy(
            src_ref=ref, dst_ref=ref, send_sem=ft_sem.at[0], recv_sem=fr_sem.at[k],
            device_id=(me, (t + 1) % nt), device_id_type=MESH,
        )

    def send_features(k):
        for j in range(1, nt):
            feature_copy(k, j).start()

    def features_in(k):
        value = products(k, 0)
        for h in range(nt // 2):
            fs[h] = value[:, 128 * h : 128 * h + 128]
            even = fs[h, pl.ds(0, 32, stride=2), :]
            odd = fs[h, pl.ds(1, 32, stride=2), :]
            ftx[k, 2 * h] = jnp.where(first, even, pltpu.roll(odd, 64, 1))
            ftx[k, 2 * h + 1] = jnp.where(first, pltpu.roll(even, 64, 1), odd)
        send_features(k)

    def features_out():
        fh[:, pl.ds(0, 64)] = products(0, 1).T
        for s in range(nt):
            even = fh[pl.ds(64 * s, 32, stride=2), :]
            odd = fh[pl.ds(64 * s + 1, 32, stride=2), :]
            ftx[0, s] = jnp.concatenate([even[:, :64], odd[:, :64]], axis=1)
        send_features(0)

    words = [jnp.where(end, jnp.int32(a), jnp.int32(b)) for a, b in zip(packed(END), packed(MID))]

    def decode(i):
        word = words[0]
        for j in range(1, len(words)):
            word = jnp.where(i // PER == j, words[j], word)
        code = lax.shift_right_logical(word, 5 * (i % PER)) % 32
        return (code // 4) % 4, code // 16 == 1, code % 4

    beside_slot = slot_of(1, False)

    def ship():
        return remote(act.at[GATE - 1, beside_slot], guest, beside_slot, PM, g_sem.at[0], inward)

    def help_back(slot):
        return remote(gtx, grx, slot, GATE, g_sem.at[1], outward)

    def send_late(p):
        part = rows_of(across, p)
        remote(part, part, across, p, w_sem.at[1], outward).start()

    def event(i, carry):
        q, other, p = decode(i)
        slot = slot_of(q, other)
        mine = jnp.logical_not(other) & (q == r)
        beside = (q - r == 1) | (r - q == 1)
        todo = jnp.logical_not(mine | ((p <= HID) & jnp.logical_not(other) & beside))
        go = tuple(todo & g for g in wanted(q, other, p))

        @pl.when(p == 0)
        def _():
            copies = model_routes(slot)

            @pl.when(todo)
            def _():
                copies[2].wait_recv()

            begin(copies, go)
            cols = pl.ds(pl.multiple_of(slot * feats, 128), feats)
            weights = pmb[slot]
            macc[0] += jnp.dot(io_v[0, :, cols], weights, preferred_element_type=F32)
            macc[1] += jnp.dot(io_v[1, :, cols], weights, preferred_element_type=F32)

        @pl.when(p > 0)
        def _():
            copies = hidden_routes(slot, p)

            helped = end & jnp.logical_not(other) & (q == 1) & (p == GATE)

            @pl.when(todo & jnp.logical_not(helped))
            def _():
                copies[2].wait_recv()

            begin(copies, go)

            @pl.when(jnp.logical_not(end) & jnp.logical_not(other) & (q == nz - 1) & (p == GATE))
            def _():
                send_late(UP)

            @pl.when(helped)
            def _():
                help_back(beside_slot).wait_recv()
                wacc[GATE - 1] += grx[...].astype(F32)

            @pl.when(jnp.logical_not(helped))
            def _():
                wacc[p - 1] += lax.dot_general(
                    rows_of(slot, p)[...], act[p - 1, slot], NT, preferred_element_type=F32
                )

        @pl.when(end & (i == SHIPPED))
        def _():
            ship().start()

        @pl.when(jnp.logical_not(end) & (i == HELPED))
        def _():
            ship().wait_recv()
            gtx[...] = lax.dot_general(
                rows_of(me, GATE)[...], guest[...], NT, preferred_element_type=F32
            ).astype(BF16)
            help_back(me).start()
            send_late(GATE)

        @pl.when(i == jnp.where(end, MODEL_SENT[0], MODEL_SENT[1]))
        def _():
            send_model()

        @pl.when(i == jnp.where(end, MODEL_SUMMED[0], MODEL_SUMMED[1]))
        def _():
            sum_model()

        @pl.when(i == jnp.where(end, HID_DONE[0], HID_DONE[1]))
        def _():
            features_out()

        at_up = i == jnp.where(end, UP_DONE[0], UP_DONE[1])

        @pl.when(at_up | (i == len(END) - 1))
        def _():
            features_in(jnp.where(at_up, 1, 2))

        return carry

    lax.fori_loop(0, len(END), event, 0)

    def all_sent(ref, sem):
        pltpu.make_async_remote_copy(
            src_ref=ref, dst_ref=ref, send_sem=sem, recv_sem=recv.at[me, PM],
            device_id=(across, t), device_id_type=MESH,
        ).wait_send()

    def sent(k, blocks, rows):
        all_sent(pmb.at[pl.ds(0, blocks)], p_sem.at[k])
        all_sent(wtb.at[pl.ds(0, rows), :], w_sem.at[k])

    @pl.when(end)
    def _():
        sent(0, 1, 384)
        sent(2, 4, 640)
        ship().wait_send()

    @pl.when(jnp.logical_not(end))
    def _():
        sent(0, 2, 384)
        sent(1, 3, 640)
        help_back(me).wait_send()
        sent(2, 4, 576)

    mate_copy.wait_send()
    far_both.wait_send()
    for k in range(3):
        total = ftx[k, t]
        feature_wait(frx.at[k], k).wait_recv()
        for j in range(1, nt):
            total = total + frx[k, j - 1]
        out[pl.ds(32 * (2, 1, 0)[k], 32), :] = total
    feature_wait(frx, 0).wait_send()


def fused(
    nz, nx, ny,
    inputs, out_grads, gate_pre, up_pre, hidden_grad, proj_model, proj_hidden, lengths, owners,
):
    ndp = nz * nx
    nt = 2 * ny
    toks, wide = inputs.shape
    units, feats = proj_hidden.shape[0], proj_model.shape[0]
    hbm = pl.BlockSpec(memory_space=pltpu.HBM)
    dma = pltpu.SemaphoreType.DMA
    out = pl.pallas_call(
        functools.partial(kernel, nz, nx, ny),
        out_shape=pltpu.VMEM((96, 128), F32),
        in_specs=[hbm] * 9,
        out_specs=pl.BlockSpec(memory_space=pltpu.VMEM),
        scratch_shapes=[
            pltpu.VMEM((ndp, 3, toks, units), BF16),
            pltpu.VMEM((3, ndp, toks, units), BF16),
            pltpu.VMEM((2, toks, wide), BF16),
            pltpu.VMEM((ndp, feats, 128), BF16),
            pltpu.VMEM((ndp * 192, units), BF16),
            pltpu.VMEM((2, toks, 128), F32),
            pltpu.VMEM((3, 64, toks), F32),
            pltpu.VMEM((toks, 128), F32),
            pltpu.VMEM((toks, 128), BF16),
            pltpu.VMEM((toks, 128), F32),
            pltpu.VMEM((2, toks, 128), BF16),
            pltpu.VMEM((2, 2, toks, 64 * nt), BF16),
            pltpu.VMEM((nt // 2, 64, 128), F32),
            pltpu.VMEM((64 * nt, 128), F32),
            pltpu.VMEM((3, nt, 32, 128), F32),
            pltpu.VMEM((3, nt - 1, 32, 128), F32),
            pltpu.VMEM((toks, units), BF16),
            pltpu.VMEM((64, toks), BF16),
            pltpu.VMEM((64, toks), BF16),
            pltpu.SMEM((1, nt), jnp.int32),
            pltpu.SMEM((1, nt), jnp.int32),
            dma((ndp,)),
            dma((1,)),
            dma((4,)),
            dma((ndp, 4)),
            dma((3,)),
            dma((3,)),
            dma((2,)),
            dma((2,)),
            dma((2,)),
            dma((1,)),
            dma((3,)),
        ],
        compiler_params=pltpu.CompilerParams(
            collective_id=0, has_side_effects=True, vmem_limit_bytes=60416 << 10
        ),
    )(inputs, out_grads, gate_pre, up_pre, hidden_grad, proj_model, proj_hidden.T, lengths, owners)
    return out.reshape(1, 3 * 64 * 64)


def per_device(
    inputs, out_grads, gate_pre, up_pre, hidden_grad, proj_model, proj_hidden, lengths, owners
):
    rank_width = proj_model.shape[1] // 2
    tok_rows = inputs.shape[0]
    gate_value = gate_pre.astype(jnp.float32)
    up_value = up_pre.astype(jnp.float32)
    grad_value = hidden_grad.astype(jnp.float32)
    sigmoid_gate = jax.nn.sigmoid(gate_value)
    hidden = (gate_value * sigmoid_gate * up_value).astype(jnp.bfloat16)
    up_grad = (grad_value * gate_value * sigmoid_gate).astype(jnp.bfloat16)
    gate_grad = (
        grad_value * up_value * sigmoid_gate * (1.0 + gate_value * (1.0 - sigmoid_gate))
    ).astype(jnp.bfloat16)
    sources = (gate_grad, up_grad, hidden)
    block_rows = lax.all_gather(proj_hidden, "dp", axis=0, tiled=True)
    parts = []
    for column, source in enumerate(sources):
        parts.append(
            jnp.dot(
                source,
                block_rows[:, column * rank_width : (column + 1) * rank_width],
                preferred_element_type=jnp.float32,
            )
        )
    hidden_part = jnp.concatenate(parts, axis=1)
    block_rows = lax.all_gather(proj_model, "dp", axis=0, tiled=True)
    first_part = jnp.dot(inputs, block_rows[:, :rank_width], preferred_element_type=jnp.float32)
    second_part = jnp.dot(out_grads, block_rows[:, rank_width:], preferred_element_type=jnp.float32)
    model_part = jnp.concatenate([first_part, second_part], axis=1)
    partial_value = jnp.concatenate([hidden_part, model_part], axis=1)
    lens = lengths[0]
    owner_row = owners[0]
    order = jnp.arange(lens.shape[0], dtype=jnp.int32)
    starts = jnp.sum(jnp.where(order[None, :] < order[:, None], lens[None, :], 0), axis=1)
    myself = lax.axis_index("tensor")
    tensor_count = lax.axis_size("tensor")
    chosen = (owner_row == myself).astype(jnp.int32)
    my_length = jnp.sum(lens * chosen)
    capacity = 3 * tok_rows // tensor_count
    slots = jnp.arange(capacity * lax.axis_size("tensor"), dtype=jnp.int32)
    holder = slots // capacity
    within = slots % capacity
    matched = (owner_row[None, :] == holder[:, None]).astype(jnp.int32)
    first_token = jnp.sum(matched * starts[None, :], axis=1)
    span = jnp.sum(matched * lens[None, :], axis=1)
    valid = within < span
    picked = jnp.where(valid, first_token + within, 0)
    summed = lax.psum_scatter(
        jnp.take(partial_value, picked, axis=0) * valid[:, None].astype(jnp.float32),
        "tensor",
        scatter_dimension=0,
        tiled=True,
    )
    weights = (jnp.arange(capacity, dtype=jnp.int32) < my_length).astype(jnp.float32)

    def block_of(index):
        return summed[:, index * rank_width : (index + 1) * rank_width]

    pairs = ((0, 3), (1, 3), (4, 2))
    blocks = []
    for left_index, right_index in pairs:
        left_side = block_of(left_index) * weights[:, None]
        blocks.append(
            jnp.einsum(
                "ta,tb->ab", left_side, block_of(right_index), precision=lax.Precision.HIGHEST
            )
        )
    return jnp.stack(blocks, axis=0).reshape(1, 3 * rank_width * rank_width)


def solution(mesh):
    in_specs = (
        P("dp", "tensor"),
        P("dp", "tensor"),
        P("dp", "tensor"),
        P("dp", "tensor"),
        P("dp", "tensor"),
        P(("tensor", "dp"), None),
        P(("tensor", "dp"), None),
        P("dp", None),
        P("dp", None),
    )
    out_specs = P(("dp", "tensor"), None)
    ndp, ny = mesh.shape["dp"], mesh.shape["tensor"] // 2

    def program(*args):
        units, feats, rank_width = args[6].shape[0], args[5].shape[0], args[5].shape[1] // 2
        nx = math.isqrt(ndp // 2)
        fits = units % 128 == 0 and feats % 128 == 0 and rank_width == 64 and args[0].shape[0] % 128 == 0
        if fits and (nx, ny) == (2, 2) and ndp == 4 * nx:
            return fused(ndp // nx, nx, ny, *args)
        return per_device(*args)

    return jax.shard_map(
        program, mesh=mesh, in_specs=in_specs, out_specs=out_specs, check_vma=False
    )
```

```python
import functools
import math

import jax
import jax.numpy as jnp
from jax import lax
from jax.experimental import pallas as pl
from jax.experimental.pallas import tpu as pltpu
from jax.sharding import PartitionSpec as P

MESH = pl.DeviceIdType.MESH
NT = (((1,), (1,)), ((), ()))
F32 = jnp.float32
BF16 = jnp.bfloat16
ROWS = 32
PM, HID, UP, GATE = range(4)
END = (
    (0, 0, PM), (0, 0, HID), (0, 1, HID), (0, 1, UP),
    (2, 0, PM), (0, 0, UP), (0, 0, GATE), (1, 0, PM),
    (1, 0, HID), (0, 1, PM), (1, 1, PM), (2, 0, HID),
    (0, 1, GATE), (2, 0, UP), (1, 1, HID), (3, 0, PM),
    (2, 1, PM), (2, 0, GATE), (2, 1, HID), (3, 0, HID),
    (2, 1, UP), (3, 0, UP), (3, 1, PM), (3, 0, GATE),
    (2, 1, GATE), (1, 0, UP), (3, 1, HID), (1, 1, UP),
    (3, 1, UP), (1, 0, GATE), (1, 1, GATE), (3, 1, GATE),
)
MID = (
    (2, 0, UP), (0, 0, UP), (1, 0, PM), (1, 0, HID),
    (3, 0, PM), (1, 0, UP), (1, 0, GATE), (0, 0, PM),
    (2, 0, PM), (0, 0, GATE), (2, 0, HID), (2, 0, GATE),
    (0, 0, HID), (1, 1, PM), (1, 1, HID), (1, 1, UP),
    (0, 1, PM), (2, 1, PM), (3, 0, HID), (1, 1, GATE),
    (0, 1, HID), (3, 0, UP), (2, 1, HID), (3, 1, PM),
    (3, 0, GATE), (2, 1, UP), (2, 1, GATE), (0, 1, UP),
    (3, 1, HID), (0, 1, GATE), (3, 1, UP), (3, 1, GATE),
)
MODEL_SENT = (22, 25)
MODEL_SUMMED = (26, 29)
HID_DONE = (26, 29)
UP_DONE = (28, 30)
SHIPPED, HELPED = 2, 26
PER = 6


def packed(events):
    words = []
    for at in range(0, len(events), PER):
        word = 0
        for j, (plane, other, piece) in enumerate(events[at : at + PER]):
            word += ((plane + 4 * other) * 4 + piece) << (5 * j)
        words.append(word)
    return words


def kernel(
    nz, nx, ny,
    inp_h, og_h, gp_h, up_h, hg_h, pm_h, wt_h, lens_h, owns_h,
    out,
    raw, act, io_v, pmb, wtb, macc, wacc, mtx, mtxb, mrx, mrxb, mm, fs, fh, ftx, frx, guest, gtx, grx, lens, owns,
    raw_sem, io_sem, own_sem, recv, w_sem, p_sem, g_sem, mt_sem, mr_sem, ft_sem, fr_sem,
):
    ndp = nz * nx
    nt = 2 * ny
    me = lax.axis_index("dp")
    t = lax.axis_index("tensor")
    z, x = me // nx, me % nx
    low_half = z < nz // 2
    r = jnp.where(low_half, z, nz - 1 - z)
    inward = me + jnp.where(low_half, nx, -nx)
    outward = me - jnp.where(low_half, nx, -nx)
    across = z * nx + 1 - x
    end = r == 0
    units = wt_h.shape[1]
    feats = pm_h.shape[0]
    toks = inp_h.shape[0]
    sources = (gp_h, up_h, hg_h)

    def raw_copy(block, q):
        cols = pl.ds(block * units, units)
        return pltpu.make_async_copy(sources[q].at[:, cols], raw.at[block, q], raw_sem.at[block])

    io = (pltpu.make_async_copy(inp_h, io_v.at[0], io_sem.at[0]),
          pltpu.make_async_copy(og_h, io_v.at[1], io_sem.at[0]))

    barrier = pltpu.get_barrier_semaphore()

    def greet(d, s):
        pl.semaphore_signal(barrier, inc=1, device_id=(d, s), device_id_type=MESH)

    greet(across, t)
    greet(inward, t)

    @pl.when(jnp.logical_not(end))
    def _():
        greet(outward, t)

    for j in range(1, nt):
        greet(me, (t + j) % nt)
    for block in range(ndp):
        for q in range(3):
            raw_copy(block, q).start()
    pl.semaphore_wait(barrier, nt + 1 + r)

    def rows_of(slot, p, first=0, count=64):
        return wtb.at[pl.ds(pl.multiple_of(slot * 192 + (3 - p) * 64 + first, 16), count), :]

    def remote(src, dst, slot, p, sem, d):
        return pltpu.make_async_remote_copy(
            src_ref=src, dst_ref=dst, send_sem=sem, recv_sem=recv.at[slot, p],
            device_id=(d, t), device_id_type=MESH,
        )

    def routes(src, dst, slot, p, sems):
        return tuple(
            remote(src, dst, slot, p, sems.at[k], d) for k, d in enumerate((inward, outward, across))
        )

    def model_routes(slot):
        return routes(pmb.at[slot], pmb.at[slot], slot, PM, p_sem)

    def hidden_routes(slot, p):
        return routes(rows_of(slot, p), rows_of(slot, p), slot, p, w_sem)

    def wanted(q, other, p):
        same = jnp.logical_not(other)
        mid = jnp.logical_not(end)
        go_in = (mid & same & (q == 0)) | (end & other & (q == 0) & (p > 0))
        go_out = mid & same & (q >= 2)
        go_x = same & ((end & ((q >= 2) | (p <= HID))) | (mid & ((q >= 2) | (p == 0))))
        return go_in, go_out, go_x

    def slot_of(q, other):
        return jnp.where(low_half, q, nz - 1 - q) * nx + jnp.where(other, 1 - x, x)

    def begin(copies, conditions):
        for copy, condition in zip(copies, conditions):
            @pl.when(condition)
            def _():
                copy.start()

    def send_own(p):
        if p is PM:
            copies = routes(pm_h, pmb.at[me], me, PM, p_sem)
        else:
            own = wt_h.at[pl.ds((3 - p) * 64, 64), :]
            copies = routes(own, rows_of(me, p), me, p, w_sem)
        if p is not GATE:
            @pl.when(jnp.logical_not(end))
            def _():
                copies[1].start()
        copies[2].start()
        copies[0].start()

    for p in (PM, HID, UP):
        send_own(p)
    keep = (
        pltpu.make_async_copy(pm_h, pmb.at[me], own_sem.at[0]),
        pltpu.make_async_copy(lens_h, lens, own_sem.at[2]),
        pltpu.make_async_copy(owns_h, owns, own_sem.at[3]),
        pltpu.make_async_copy(wt_h, wtb.at[pl.ds(pl.multiple_of(me * 192, 64), 192), :], own_sem.at[1]),
    )
    for copy in keep:
        copy.start()
    for copy in io:
        copy.start()
    macc[...] = jnp.zeros_like(macc)
    wacc[...] = jnp.zeros_like(wacc)

    def near(q, p):
        slot = slot_of(q, False)
        copies = model_routes(slot) if p is PM else hidden_routes(slot, p)
        copies[2].wait_recv()
        begin(copies, wanted(jnp.int32(q), False, p))

    def elementwise(block, carry):
        for at, p in ((ndp // 2, PM), (3 * ndp // 4, HID)):
            @pl.when((block == at) & end)
            def _():
                near(1, p)

            @pl.when((block == at) & jnp.logical_not(end))
            def _():
                near(2, p)
                near(0, p)

        @pl.when(block == ndp // 2)
        def _():
            send_own(GATE)

        pltpu.make_async_copy(raw.at[block], raw.at[block], raw_sem.at[block]).wait()

        def some(i, carry):
            rows = pl.ds(pl.multiple_of(i * ROWS, ROWS), ROWS)
            gate = raw[block, 0, rows, :].astype(F32)
            up = raw[block, 1, rows, :].astype(F32)
            grad = raw[block, 2, rows, :].astype(F32)
            sig = 0.5 * jnp.tanh(0.5 * gate) + 0.5
            silu = gate * sig
            act[0, block, rows, :] = (silu * up).astype(BF16)
            act[1, block, rows, :] = (grad * silu).astype(BF16)
            act[2, block, rows, :] = (grad * up * (sig + silu * (1.0 - sig))).astype(BF16)
            return carry

        lax.fori_loop(0, toks // ROWS, some, 0)
        return carry

    lax.fori_loop(0, ndp, elementwise, 0)
    pltpu.make_async_copy(io_v, io_v, io_sem.at[0]).wait()
    for copy in keep:
        copy.wait()

    first_lanes = lax.broadcasted_iota(jnp.int32, (toks, 128), 1) < 64
    first = lax.broadcasted_iota(jnp.int32, (32, 128), 1) < 64

    c = t % 2
    y = t // 2
    mate_copy = pltpu.make_async_remote_copy(
        src_ref=mtx, dst_ref=mrx, send_sem=mt_sem.at[0], recv_sem=mr_sem.at[0],
        device_id=(me, y * 2 + 1 - c), device_id_type=MESH,
    )
    far_copies = [
        pltpu.make_async_remote_copy(
            src_ref=mtxb, dst_ref=mrxb.at[j], send_sem=mt_sem.at[1], recv_sem=mr_sem.at[1],
            device_id=(me, (1 - y) * 2 + (c + j) % 2), device_id_type=MESH,
        )
        for j in range(2)
    ]
    far_both = pltpu.make_async_remote_copy(
        src_ref=mrxb, dst_ref=mrxb, send_sem=mt_sem.at[1], recv_sem=mr_sem.at[1],
        device_id=(me, (1 - y) * 2 + c), device_id_type=MESH,
    )

    def send_model():
        both = jnp.where(first_lanes, macc[0], macc[1])
        mtx[...] = both
        mtxb[...] = both.astype(BF16)
        for copy in far_copies:
            copy.start()
        mate_copy.start()

    def sum_model():
        mate_copy.wait_recv()
        far_both.wait_recv()
        full = mtx[...] + mrx[...] + (mrxb[0].astype(F32) + mrxb[1].astype(F32))
        turned = pltpu.roll(full, 64, 1)
        pair = (jnp.where(first_lanes, full, turned), jnp.where(first_lanes, turned, full))
        starts, stops = [], []
        for s in range(nt):
            start, stop, seen = jnp.int32(0), jnp.int32(0), jnp.int32(0)
            for e in range(nt):
                hit = owns[0, e] == s
                start = jnp.where(hit, seen, start)
                seen = seen + lens[0, e]
                stop = jnp.where(hit, seen, stop)
            starts.append(start)
            stops.append(stop)
        token = lax.broadcasted_iota(jnp.int32, (toks, 128), 0)
        for h in range(nt // 2):
            start = jnp.where(first_lanes, starts[2 * h], starts[2 * h + 1])
            stop = jnp.where(first_lanes, stops[2 * h], stops[2 * h + 1])
            inside = (token >= start) & (token < stop)
            for side in range(2):
                value = jnp.where(inside, pair[side], 0.0)
                high = value.astype(BF16)
                mm[side, 0, :, pl.ds(128 * h, 128)] = high
                mm[side, 1, :, pl.ds(128 * h, 128)] = (value - high.astype(F32)).astype(BF16)

    def products(k, side):
        value = wacc[k]
        high = value.astype(BF16)
        rest = (value - high.astype(F32)).astype(BF16)

        def dot(left, right):
            return jnp.dot(left, right, preferred_element_type=F32)

        return dot(high, mm[side, 0]) + (dot(high, mm[side, 1]) + dot(rest, mm[side, 0]))

    def feature_copy(k, j):
        s = (t + j) % nt
        return pltpu.make_async_remote_copy(
            src_ref=ftx.at[k, s], dst_ref=frx.at[k, j - 1], send_sem=ft_sem.at[0],
            recv_sem=fr_sem.at[k], device_id=(me, s), device_id_type=MESH,
        )

    def feature_wait(ref, k):
        return pltpu.make_async_remote_copy(
            src_ref=ref, dst_ref=ref, send_sem=ft_sem.at[0], recv_sem=fr_sem.at[k],
            device_id=(me, (t + 1) % nt), device_id_type=MESH,
        )

    def send_features(k):
        for j in range(1, nt):
            feature_copy(k, j).start()

    def features_in(k):
        value = products(k, 0)
        for h in range(nt // 2):
            fs[h] = value[:, 128 * h : 128 * h + 128]
            even = fs[h, pl.ds(0, 32, stride=2), :]
            odd = fs[h, pl.ds(1, 32, stride=2), :]
            ftx[k, 2 * h] = jnp.where(first, even, pltpu.roll(odd, 64, 1))
            ftx[k, 2 * h + 1] = jnp.where(first, pltpu.roll(even, 64, 1), odd)
        send_features(k)

    def features_out():
        fh[:, pl.ds(0, 64)] = products(0, 1).T
        for s in range(nt):
            even = fh[pl.ds(64 * s, 32, stride=2), :]
            odd = fh[pl.ds(64 * s + 1, 32, stride=2), :]
            ftx[0, s] = jnp.concatenate([even[:, :64], odd[:, :64]], axis=1)
        send_features(0)

    words = [jnp.where(end, jnp.int32(a), jnp.int32(b)) for a, b in zip(packed(END), packed(MID))]

    def decode(i):
        word = words[0]
        for j in range(1, len(words)):
            word = jnp.where(i // PER == j, words[j], word)
        code = lax.shift_right_logical(word, 5 * (i % PER)) % 32
        return (code // 4) % 4, code // 16 == 1, code % 4

    beside_slot = slot_of(1, False)

    def ship():
        return remote(act.at[GATE - 1, beside_slot], guest, beside_slot, PM, g_sem.at[0], inward)

    def help_back(slot):
        return remote(gtx, grx, slot, GATE, g_sem.at[1], outward)

    def send_late(p):
        part = rows_of(across, p)
        remote(part, part, across, p, w_sem.at[1], outward).start()

    def event(i, carry):
        q, other, p = decode(i)
        slot = slot_of(q, other)
        mine = jnp.logical_not(other) & (q == r)
        beside = (q - r == 1) | (r - q == 1)
        todo = jnp.logical_not(mine | ((p <= HID) & jnp.logical_not(other) & beside))
        go = tuple(todo & g for g in wanted(q, other, p))

        @pl.when(p == 0)
        def _():
            copies = model_routes(slot)

            @pl.when(todo)
            def _():
                copies[2].wait_recv()

            begin(copies, go)
            cols = pl.ds(pl.multiple_of(slot * feats, 128), feats)
            weights = pmb[slot]
            macc[0] += jnp.dot(io_v[0, :, cols], weights, preferred_element_type=F32)
            macc[1] += jnp.dot(io_v[1, :, cols], weights, preferred_element_type=F32)

        @pl.when(p > 0)
        def _():
            copies = hidden_routes(slot, p)

            helped = end & jnp.logical_not(other) & (q == 1) & (p == GATE)

            @pl.when(todo & jnp.logical_not(helped))
            def _():
                copies[2].wait_recv()

            begin(copies, go)

            @pl.when(jnp.logical_not(end) & jnp.logical_not(other) & (q == nz - 1) & (p == GATE))
            def _():
                send_late(UP)

            @pl.when(helped)
            def _():
                help_back(beside_slot).wait_recv()
                wacc[GATE - 1] += grx[...].astype(F32)

            @pl.when(jnp.logical_not(helped))
            def _():
                wacc[p - 1] += lax.dot_general(
                    rows_of(slot, p)[...], act[p - 1, slot], NT, preferred_element_type=F32
                )

        @pl.when(end & (i == SHIPPED))
        def _():
            ship().start()

        @pl.when(jnp.logical_not(end) & (i == HELPED))
        def _():
            ship().wait_recv()
            gtx[...] = lax.dot_general(
                rows_of(me, GATE)[...], guest[...], NT, preferred_element_type=F32
            ).astype(BF16)
            help_back(me).start()
            send_late(GATE)

        @pl.when(i == jnp.where(end, MODEL_SENT[0], MODEL_SENT[1]))
        def _():
            send_model()

        @pl.when(i == jnp.where(end, MODEL_SUMMED[0], MODEL_SUMMED[1]))
        def _():
            sum_model()

        @pl.when(i == jnp.where(end, HID_DONE[0], HID_DONE[1]))
        def _():
            features_out()

        at_up = i == jnp.where(end, UP_DONE[0], UP_DONE[1])

        @pl.when(at_up | (i == len(END) - 1))
        def _():
            features_in(jnp.where(at_up, 1, 2))

        return carry

    lax.fori_loop(0, len(END), event, 0)

    def all_sent(ref, sem):
        pltpu.make_async_remote_copy(
            src_ref=ref, dst_ref=ref, send_sem=sem, recv_sem=recv.at[me, PM],
            device_id=(across, t), device_id_type=MESH,
        ).wait_send()

    def sent(k, blocks, rows):
        all_sent(pmb.at[pl.ds(0, blocks)], p_sem.at[k])
        all_sent(wtb.at[pl.ds(0, rows), :], w_sem.at[k])

    @pl.when(end)
    def _():
        sent(0, 1, 384)
        sent(2, 4, 640)
        ship().wait_send()

    @pl.when(jnp.logical_not(end))
    def _():
        sent(0, 2, 384)
        sent(1, 3, 640)
        help_back(me).wait_send()
        sent(2, 4, 576)

    mate_copy.wait_send()
    far_both.wait_send()
    for k in range(3):
        total = ftx[k, t]
        feature_wait(frx.at[k], k).wait_recv()
        for j in range(1, nt):
            total = total + frx[k, j - 1]
        out[pl.ds(32 * (2, 1, 0)[k], 32), :] = total
    feature_wait(frx, 0).wait_send()


def fused(
    nz, nx, ny,
    inputs, out_grads, gate_pre, up_pre, hidden_grad, proj_model, proj_hidden, lengths, owners,
):
    ndp = nz * nx
    nt = 2 * ny
    toks, wide = inputs.shape
    units, feats = proj_hidden.shape[0], proj_model.shape[0]
    hbm = pl.BlockSpec(memory_space=pltpu.HBM)
    dma = pltpu.SemaphoreType.DMA
    out = pl.pallas_call(
        functools.partial(kernel, nz, nx, ny),
        out_shape=pltpu.VMEM((96, 128), F32),
        in_specs=[hbm] * 9,
        out_specs=pl.BlockSpec(memory_space=pltpu.VMEM),
        scratch_shapes=[
            pltpu.VMEM((ndp, 3, toks, units), BF16),
            pltpu.VMEM((3, ndp, toks, units), BF16),
            pltpu.VMEM((2, toks, wide), BF16),
            pltpu.VMEM((ndp, feats, 128), BF16),
            pltpu.VMEM((ndp * 192, units), BF16),
            pltpu.VMEM((2, toks, 128), F32),
            pltpu.VMEM((3, 64, toks), F32),
            pltpu.VMEM((toks, 128), F32),
            pltpu.VMEM((toks, 128), BF16),
            pltpu.VMEM((toks, 128), F32),
            pltpu.VMEM((2, toks, 128), BF16),
            pltpu.VMEM((2, 2, toks, 64 * nt), BF16),
            pltpu.VMEM((nt // 2, 64, 128), F32),
            pltpu.VMEM((64 * nt, 128), F32),
            pltpu.VMEM((3, nt, 32, 128), F32),
            pltpu.VMEM((3, nt - 1, 32, 128), F32),
            pltpu.VMEM((toks, units), BF16),
            pltpu.VMEM((64, toks), BF16),
            pltpu.VMEM((64, toks), BF16),
            pltpu.SMEM((1, nt), jnp.int32),
            pltpu.SMEM((1, nt), jnp.int32),
            dma((ndp,)),
            dma((1,)),
            dma((4,)),
            dma((ndp, 4)),
            dma((3,)),
            dma((3,)),
            dma((2,)),
            dma((2,)),
            dma((2,)),
            dma((1,)),
            dma((3,)),
        ],
        compiler_params=pltpu.CompilerParams(
            collective_id=0, has_side_effects=True, vmem_limit_bytes=60416 << 10
        ),
    )(inputs, out_grads, gate_pre, up_pre, hidden_grad, proj_model, proj_hidden.T, lengths, owners)
    return out.reshape(1, 3 * 64 * 64)


def per_device(
    inputs, out_grads, gate_pre, up_pre, hidden_grad, proj_model, proj_hidden, lengths, owners
):
    rank_width = proj_model.shape[1] // 2
    tok_rows = inputs.shape[0]
    gate_value = gate_pre.astype(jnp.float32)
    up_value = up_pre.astype(jnp.float32)
    grad_value = hidden_grad.astype(jnp.float32)
    sigmoid_gate = jax.nn.sigmoid(gate_value)
    hidden = (gate_value * sigmoid_gate * up_value).astype(jnp.bfloat16)
    up_grad = (grad_value * gate_value * sigmoid_gate).astype(jnp.bfloat16)
    gate_grad = (
        grad_value * up_value * sigmoid_gate * (1.0 + gate_value * (1.0 - sigmoid_gate))
    ).astype(jnp.bfloat16)
    sources = (gate_grad, up_grad, hidden)
    block_rows = lax.all_gather(proj_hidden, "dp", axis=0, tiled=True)
    parts = []
    for column, source in enumerate(sources):
        parts.append(
            jnp.dot(
                source,
                block_rows[:, column * rank_width : (column + 1) * rank_width],
                preferred_element_type=jnp.float32,
            )
        )
    hidden_part = jnp.concatenate(parts, axis=1)
    block_rows = lax.all_gather(proj_model, "dp", axis=0, tiled=True)
    first_part = jnp.dot(inputs, block_rows[:, :rank_width], preferred_element_type=jnp.float32)
    second_part = jnp.dot(out_grads, block_rows[:, rank_width:], preferred_element_type=jnp.float32)
    model_part = jnp.concatenate([first_part, second_part], axis=1)
    partial_value = jnp.concatenate([hidden_part, model_part], axis=1)
    lens = lengths[0]
    owner_row = owners[0]
    order = jnp.arange(lens.shape[0], dtype=jnp.int32)
    starts = jnp.sum(jnp.where(order[None, :] < order[:, None], lens[None, :], 0), axis=1)
    myself = lax.axis_index("tensor")
    tensor_count = lax.axis_size("tensor")
    chosen = (owner_row == myself).astype(jnp.int32)
    my_length = jnp.sum(lens * chosen)
    capacity = 3 * tok_rows // tensor_count
    slots = jnp.arange(capacity * lax.axis_size("tensor"), dtype=jnp.int32)
    holder = slots // capacity
    within = slots % capacity
    matched = (owner_row[None, :] == holder[:, None]).astype(jnp.int32)
    first_token = jnp.sum(matched * starts[None, :], axis=1)
    span = jnp.sum(matched * lens[None, :], axis=1)
    valid = within < span
    picked = jnp.where(valid, first_token + within, 0)
    summed = lax.psum_scatter(
        jnp.take(partial_value, picked, axis=0) * valid[:, None].astype(jnp.float32),
        "tensor",
        scatter_dimension=0,
        tiled=True,
    )
    weights = (jnp.arange(capacity, dtype=jnp.int32) < my_length).astype(jnp.float32)

    def block_of(index):
        return summed[:, index * rank_width : (index + 1) * rank_width]

    pairs = ((0, 3), (1, 3), (4, 2))
    blocks = []
    for left_index, right_index in pairs:
        left_side = block_of(left_index) * weights[:, None]
        blocks.append(
            jnp.einsum(
                "ta,tb->ab", left_side, block_of(right_index), precision=lax.Precision.HIGHEST
            )
        )
    return jnp.stack(blocks, axis=0).reshape(1, 3 * rank_width * rank_width)


def solution(mesh):
    in_specs = (
        P("dp", "tensor"),
        P("dp", "tensor"),
        P("dp", "tensor"),
        P("dp", "tensor"),
        P("dp", "tensor"),
        P(("tensor", "dp"), None),
        P(("tensor", "dp"), None),
        P("dp", None),
        P("dp", None),
    )
    out_specs = P(("dp", "tensor"), None)
    ndp, ny = mesh.shape["dp"], mesh.shape["tensor"] // 2

    def program(*args):
        units, feats, rank_width = args[6].shape[0], args[5].shape[0], args[5].shape[1] // 2
        nx = math.isqrt(ndp // 2)
        fits = units % 128 == 0 and feats % 128 == 0 and rank_width == 64 and args[0].shape[0] % 128 == 0
        if fits and (nx, ny) == (2, 2) and ndp == 4 * nx:
            return fused(ndp // nx, nx, ny, *args)
        return per_device(*args)

    return jax.shard_map(
        program, mesh=mesh, in_specs=in_specs, out_specs=out_specs, check_vma=False
    )
```
